512 devices in a mesh: grp: 16 (over x, y), frm: 32 (over z, core).
Axes of the slice: x: 4, y: 4, z: 16, core: 2. Of those that a mesh axis runs over, the one named last changes fastest.
Arguments:
- query_in: bfloat16 [32, 2048, 2048], P(None, ('grp', 'frm')), may hold values from -32 to 32
- key_in: bfloat16 [32, 2048, 2048], P(None, ('grp', 'frm')), may hold values from -32 to 32
- value_in: bfloat16 [32, 2048, 2048], P(None, ('grp', 'frm')), may hold values from -6 to 6
- cotangent: bfloat16 [32, 2048, 2048], P('frm', 'grp'), may hold values from -6 to 6
- w_in: bfloat16 [16, 2048, 4096], P('grp', None, 'frm'), may hold values from -0.25 to 0.25
- w_out: bfloat16 [16, 4096, 2048], P('grp', 'frm'), may hold values from -0.125 to 0.125
- gate_probs: float32 [8, 512], replicated, may hold values from 0.5 to 1
- chosen: int32 [8, 512], replicated, may hold values from 0 to 65535, as said below
Outputs:
- grad_query: bfloat16 [32, 2048, 2048], P(None, ('grp', 'frm'))
- grad_key: bfloat16 [32, 2048, 2048], P(None, ('grp', 'frm'))
- grad_value: bfloat16 [32, 2048, 2048], P(None, ('grp', 'frm'))
The draws below stay inside these ranges and needn't reach their ends.
Inputs may be any that keep to these rules, and one draw needn't show every extreme that they name: `chosen`: row e lists 512 distinct tokens, token t = frame * 2048 + patch. Call the tokens of 4 consecutive patches starting at a multiple of 4, over all frames, a block: an expert takes at most 2 tokens of a block, and exactly 2 of some block in every row.
All inputs are finite; a program needn't handle non-finite values.
Results may differ from the reference program's by a relative error of at most 0.025.
Values may be sent and summed in bfloat16 or wider, within the bound.
A program may use at most 64 MiB of HBM per device.

```python
import math
import jax
import jax.numpy as jnp
from jax import lax

D = 2048
F = 8192
HEADS = 16
MOST = 2
PB = 4
FRAMES = 32
PATCHES = 2048
EXPERTS = 8
CAP = 512
N_FRM = 32


def draw_query_in(key, part):
    drawn = jax.random.truncated_normal(jax.random.fold_in(key, 1), -4.0, 4.0, (FRAMES, PATCHES, HEADS, D // HEADS), jnp.float32)
    return drawn.reshape(FRAMES, PATCHES, D).astype(jnp.bfloat16)


def draw_key_in(key, part):
    drawn = jax.random.truncated_normal(jax.random.fold_in(key, 2), -4.0, 4.0, (FRAMES, PATCHES, HEADS, D // HEADS), jnp.float32)
    return drawn.reshape(FRAMES, PATCHES, D).astype(jnp.bfloat16)


def draw_chosen(key, part):
    base = jax.random.fold_in(key, 3)
    streams = jax.random.split(base, 3)
    block_total = PATCHES // PB
    local_rows = FRAMES * PB
    noise = jax.random.randint(streams[0], (EXPERTS, block_total), 0, 1 << 20) * block_total + jnp.arange(block_total)[None, :]
    ranking = jnp.argsort(jnp.argsort(noise, axis=1), axis=1)
    doubled = jax.random.randint(streams[1], (EXPERTS, 1), 1, block_total // 2 + 1)
    counts = 1 + (ranking < doubled).astype(jnp.int32) - ((ranking >= doubled) & (ranking < 2 * doubled)).astype(jnp.int32)
    spread = jax.random.randint(streams[2], (EXPERTS, block_total, local_rows), 0, 1 << 16) * local_rows + jnp.arange(local_rows)[None, None, :]
    locals_picked = jnp.argsort(spread, axis=2)[:, :, :MOST]
    frame_of = locals_picked // PB
    within = locals_picked % PB
    token_ids = frame_of * PATCHES + jnp.arange(block_total)[None, :, None] * PB + within
    alive = jnp.arange(MOST)[None, None, :] < counts[:, :, None]
    flat_tokens = token_ids.reshape(EXPERTS, block_total * MOST)
    flat_alive = alive.reshape(EXPERTS, block_total * MOST).astype(jnp.int32)
    sort_keys = (1 - flat_alive) * (block_total * MOST) + jnp.arange(block_total * MOST)[None, :]
    keeping = jnp.argsort(sort_keys, axis=1)[:, :CAP]
    return jnp.take_along_axis(flat_tokens, keeping, axis=1).astype(jnp.int32)


def strengthened(drawn, own_key, source, target, blocks, factor):
    def block_of(axis_at):
        return (jnp.arange(drawn.shape[axis_at]) // (drawn.shape[axis_at] // blocks)).reshape((-1,) + (1,) * (drawn.ndim - 1 - axis_at))

    one_side = jax.random.permutation(own_key, blocks)[block_of(target)]
    second = (block_of(target) + blocks // 2) % blocks
    return jnp.where((block_of(source) == one_side) | (block_of(source) == second), factor * drawn, drawn)


def steps_of(own_key, extent, cuts, low, top_value):
    def one(dim, parts):
        steps = jax.random.uniform(jax.random.fold_in(jax.random.fold_in(own_key, 6), dim), (parts,), jnp.float32, low / len(cuts), top_value / len(cuts))
        return jnp.repeat(jnp.exp(steps), extent[dim] // parts).reshape((-1,) + (1,) * (len(extent) - dim - 1))

    loudness = one(*cuts[0])
    for cut in cuts[1:]:
        loudness = loudness * one(*cut)
    return loudness


def bell_draw(stream_key, extent, scale, reach, cuts=(), kind=jnp.bfloat16):
    array = jax.random.normal(stream_key, extent, jnp.float32) * scale
    if len(cuts) > 0:
        array = steps_of(stream_key, extent, cuts, -0.22, 0.18) * array
    return jnp.clip(array, min=-reach, max=reach).astype(kind)


def noise_with(own_key, extent, scale, bound, cuts, heavy, kind=jnp.bfloat16):
    array = scale * jax.random.normal(own_key, extent, jnp.float32)
    if cuts:
        array = array * steps_of(own_key, extent, cuts, -0.22, 0.18)
    return jnp.clip(strengthened(array, jax.random.fold_in(own_key, 3), *heavy), -bound, bound).astype(kind)


def setup_inputs(seed: int = 0) -> dict:
    key_of = jax.random.split(jax.random.key(seed), 9)
    query_in = draw_query_in(jax.random.fold_in(key_of[8], 71), 0)
    key_in = draw_key_in(jax.random.fold_in(key_of[8], 71), 0)
    value_in = bell_draw(key_of[2], (FRAMES, PATCHES, D), 1.0, 6.0, ((1, 512),))
    cotangent = bell_draw(key_of[3], (FRAMES, PATCHES, D), 1.0, 6.0, ((0, 32), (1, 16)))
    w_in = noise_with(key_of[4], (2 * EXPERTS, D, F // 2), D ** -0.5, 0.25, ((0, 16), (2, 32)), (2, 1, 32, 2.75))
    w_out = bell_draw(key_of[5], (2 * EXPERTS, F // 2, D), D ** -0.5, 0.125, ((0, 16), (1, 32)))
    gate_probs = jnp.clip(jax.random.uniform(key_of[6], (EXPERTS, CAP), jnp.float32, 0.5, 1.0), 0.5, 1.0)
    chosen = draw_chosen(jax.random.fold_in(key_of[8], 71), 0)
    return dict(query_in=query_in, key_in=key_in, value_in=value_in, cotangent=cotangent, w_in=w_in, w_out=w_out, gate_probs=gate_probs, chosen=chosen)


root_half = 0.7071067811865476
inv_root_tau = 0.3989422804014327

def gelu_slope(pre_act):
    normal_cdf = 0.5 * (1.0 + jax.scipy.special.erf(pre_act * root_half))
    density = jnp.exp(-0.5 * pre_act * pre_act) * inv_root_tau
    return normal_cdf + pre_act * density

def softmax_rows(scores):
    highest = lax.optimization_barrier(jnp.max(scores, axis=-1, keepdims=True))
    raised = jnp.exp(scores - highest)
    return raised / lax.optimization_barrier(jnp.sum(raised, axis=-1, keepdims=True))

def round_half(values):
    return lax.optimization_barrier(values.astype(jnp.bfloat16)).astype(jnp.float32)

def reference(query_in, key_in, value_in, cotangent, w_in, w_out, gate_probs, chosen):
    frames, patches, features = query_in.shape
    head_dim = features // HEADS
    scaling = head_dim ** (-0.5)
    tokens = frames * patches
    block_size = math.gcd(patches, 64)
    block_count = patches // block_size

    def to_blocks(values):
        return values.reshape(frames, block_count, block_size, HEADS, head_dim).transpose(1, 0, 2, 3, 4)

    def from_blocks(values):
        return values.transpose(1, 0, 2, 3, 4).reshape(frames, patches, features)
    query_blocks = to_blocks(query_in)
    key_blocks = to_blocks(key_in)
    value_blocks = to_blocks(value_in)

    def probabilities(query_part, key_part):
        scores = jnp.einsum('fphd,gphd->phfg', query_part.astype(jnp.float32), key_part.astype(jnp.float32)) * scaling
        return softmax_rows(scores)

    def forward(operands):
        query_part, key_part, value_part = operands
        weights = round_half(probabilities(query_part, key_part))
        mixed = jnp.einsum('phfg,gphd->fphd', weights, value_part.astype(jnp.float32))
        return mixed.astype(jnp.bfloat16)
    attn_out = from_blocks(lax.map(forward, (query_blocks, key_blocks, value_blocks))).reshape(tokens, features)
    cot_flat = cotangent.reshape(tokens, features)
    slices = 2 * N_FRM
    slice_width = w_in.shape[2] // N_FRM
    pair_in = w_in.reshape(EXPERTS, 2, features, w_in.shape[2])
    pair_out = w_out.reshape(EXPERTS, 2, w_out.shape[1], features)

    def expert_grad(operands):
        halves_in, halves_out, probs_row, picked = operands
        hidden_in = jnp.concatenate([halves_in[0], halves_in[1]], axis=1)
        hidden_out = jnp.concatenate([halves_out[0], halves_out[1]], axis=0)
        picked = picked.astype(jnp.int32)
        rows_in = attn_out[picked]
        rows_cot = cot_flat[picked]
        scaled = (probs_row[:, None] * rows_cot.astype(jnp.float32)).astype(jnp.bfloat16)
        pre_act = jnp.dot(rows_in, hidden_in, preferred_element_type=jnp.float32)
        back_act = jnp.dot(scaled, hidden_out.T, preferred_element_type=jnp.float32)
        slope = (back_act * gelu_slope(pre_act)).astype(jnp.bfloat16)
        row_count = picked.shape[0]
        products = jnp.einsum('rsk,dsk->srd', slope.reshape(row_count, slices, slice_width).astype(jnp.float32), hidden_in.reshape(features, slices, slice_width).astype(jnp.float32))
        products = round_half(products)
        halves = lax.optimization_barrier(jnp.sum(products.reshape(2, N_FRM, row_count, features), axis=1))
        halves = round_half(halves)
        return halves[0] + halves[1]
    added = lax.map(expert_grad, (pair_in, pair_out, gate_probs, chosen))
    stream = cot_flat.astype(jnp.float32).at[chosen.reshape(-1).astype(jnp.int32)].add(added.reshape(-1, features))
    stream = stream.astype(jnp.bfloat16)
    stream_blocks = to_blocks(stream.reshape(frames, patches, features))

    def backward(operands):
        query_part, key_part, value_part, grad_part = operands
        attn_probs = probabilities(query_part, key_part)
        weights = round_half(attn_probs)
        grad_heads = grad_part.astype(jnp.float32)
        grad_value = jnp.einsum('phfg,fphd->gphd', weights, grad_heads).astype(jnp.bfloat16)
        grad_prob = jnp.einsum('fphd,gphd->phfg', grad_heads, value_part.astype(jnp.float32))
        centre = lax.optimization_barrier(jnp.sum(attn_probs * grad_prob, axis=-1, keepdims=True))
        grad_score = round_half(attn_probs * (grad_prob - centre))
        grad_query = (jnp.einsum('phfg,gphd->fphd', grad_score, key_part.astype(jnp.float32)) * scaling).astype(jnp.bfloat16)
        grad_key = (jnp.einsum('phfg,fphd->gphd', grad_score, query_part.astype(jnp.float32)) * scaling).astype(jnp.bfloat16)
        return (grad_query, grad_key, grad_value)
    grad_query, grad_key, grad_value = lax.map(backward, (query_blocks, key_blocks, value_blocks, stream_blocks))
    return (from_blocks(grad_query), from_blocks(grad_key), from_blocks(grad_value))
```

```python
import functools

import jax
import jax.numpy as jnp
from jax import lax
from jax.experimental import pallas as pl
from jax.experimental.pallas import tpu as pltpu
from jax.sharding import PartitionSpec as P

HEADS = 16
MOST = 2
MESH = pl.DeviceIdType.MESH

root_half = 0.7071067811865476
inv_root_tau = 0.3989422804014327


def gelu_slope(pre_act):
    normal_cdf = 0.5 * (1.0 + lax.erf(pre_act * root_half))
    density = jnp.exp(-0.5 * pre_act * pre_act) * inv_root_tau
    return normal_cdf + pre_act * density


NT_DIMS = (((1,), (1,)), ((), ()))


def expert_kernel(
    levels,
    rows_ref, w_in_ref, w_out_ref, out_ref,
    gathered, w1, w2, own, x_send, x_recv, slopes, parts, cross, ring_in, ring_out,
    last_in, last_total, last_cross,
    local_sem, weight_send, weight_recv, first_send, first_recv,
    ring_send, ring_recv, core_send, core_recv, x_send_sem, x_recv_sem,
    slope_send, slope_recv, part_send, part_recv, back_send, back_recv, last_send, last_recv,
):
    steps = levels // 2
    share = rows_ref.shape[1]
    block = 2 * share
    half = rows_ref.shape[2]
    hidden = w_in_ref.shape[1]
    grp = lax.axis_index("grp")
    frm = lax.axis_index("frm")
    side = lax.rem(grp, 2)
    core = lax.rem(frm, 2)
    level = lax.div(frm, 2)
    turn = 1 - 2 * core
    ahead = (grp, lax.rem(level + turn + levels, levels) * 2 + core)
    behind = (grp, lax.rem(level - turn + levels, levels) * 2 + core)
    twin = (grp, frm + turn)
    mate = (grp + 1 - 2 * side, frm)

    def remote(src, dst, send, recv, device):
        return pltpu.make_async_remote_copy(
            src_ref=src, dst_ref=dst, send_sem=send, recv_sem=recv, device_id=device, device_id_type=MESH
        )

    barrier = pltpu.get_barrier_semaphore()
    for other in (ahead, behind, twin, mate):
        pl.semaphore_signal(barrier, inc=1, device_id=other, device_id_type=MESH)

    mine = pl.ds(pl.multiple_of(side * half, half), half)
    theirs = pl.ds(pl.multiple_of((1 - side) * half, half), half)
    here = pl.ds(pl.multiple_of(core * share, share), share)
    lane = pl.ds(pl.multiple_of(core * block, block), block)
    other_lane = pl.ds(pl.multiple_of((1 - core) * block, block), block)
    lane_part = pl.ds(pl.multiple_of(core * (block + share), share), share)
    far = pl.ds(pl.multiple_of(block + core * share, share), share)
    other_far = pl.ds(pl.multiple_of(block + (1 - core) * share, share), share)
    last = steps - 1

    local = [
        pltpu.make_async_copy(rows_ref.at[0], gathered.at[0, last, here], local_sem.at[0]),
        pltpu.make_async_copy(rows_ref.at[1], gathered.at[1, last, here], local_sem.at[1]),
        pltpu.make_async_copy(w_in_ref.at[mine], w1.at[:, pl.ds(0, hidden)], local_sem.at[2]),
        pltpu.make_async_copy(w_out_ref.at[:, mine], w2.at[pl.ds(0, hidden)], local_sem.at[3]),
    ]
    for copy in local:
        copy.start()
    ring_in[last - 1] = jnp.zeros(ring_in.shape[1:], ring_in.dtype)

    pl.semaphore_wait(barrier, 4)

    first = [
        remote(rows_ref.at[a], gathered.at[a, last, here], first_send.at[a], first_recv.at[a], twin)
        for a in range(2)
    ]
    for copy in first:
        copy.start()
    weights = [
        remote(w_in_ref.at[theirs], w1.at[:, pl.ds(hidden, hidden)], weight_send.at[0], weight_recv.at[0], mate),
        remote(w_out_ref.at[:, theirs], w2.at[pl.ds(hidden, hidden)], weight_send.at[1], weight_recv.at[1], mate),
    ]
    for copy in weights:
        copy.start()

    def ring(t, a):
        return remote(
            gathered.at[a, lax.max(t - 1, 0), lane], gathered.at[a, t, lane], ring_send.at[t, a], ring_recv.at[t, a], ahead
        )

    def ring_first(a):
        return remote(
            gathered.at[a, last, pl.ds(0, block)], gathered.at[a, 0, lane],
            ring_send.at[0, a], ring_recv.at[0, a], ahead,
        )

    def ring_last(a):
        return remote(
            gathered.at[a, last - 1, lane_part], gathered.at[a, last, far],
            ring_send.at[last, a], ring_recv.at[last, a], ahead,
        )

    def core_copy(t, a):
        return remote(
            gathered.at[a, t, lane], gathered.at[a, t, lane], core_send.at[t, a], core_recv.at[t, a], twin
        )

    def core_last(a):
        return remote(
            gathered.at[a, last, far], gathered.at[a, last, far],
            core_send.at[last, a], core_recv.at[last, a], twin,
        )

    def x_copy(t):
        return remote(x_send.at[t], x_recv.at[t], x_send_sem.at[t], x_recv_sem.at[t], mate)

    def slope_copy(t):
        return remote(
            slopes.at[t, :, pl.ds(0, hidden)], slopes.at[t, :, pl.ds(hidden, hidden)],
            slope_send.at[t], slope_recv.at[t], mate,
        )

    def part_copy(t):
        return remote(parts.at[t, other_lane], cross.at[t], part_send.at[t], part_recv.at[t], twin)

    def part_last():
        return remote(
            parts.at[last, other_far], cross.at[last, pl.ds(0, share)],
            part_send.at[last], part_recv.at[last], twin,
        )

    for a in range(2):
        local[a].wait()
        first[a].wait_recv()
        ring_first(a).start()
    for copy in local[2:]:
        copy.wait()

    def multiply(t):
        pre = jnp.dot(gathered[0, t], w1[...], preferred_element_type=jnp.float32)
        own[t, 0] = pre[:, :hidden]
        x_send[t, 0] = pre[:, hidden:].astype(jnp.bfloat16)
        back = lax.dot_general(gathered[1, t], w2[...], NT_DIMS, preferred_element_type=jnp.float32)
        own[t, 1] = back[:, :hidden]
        x_send[t, 1] = back[:, hidden:].astype(jnp.bfloat16)
        x_copy(t).start()

    def bend(t):
        x_copy(t).wait_recv()
        pre = own[t, 0] + x_recv[t, 0].astype(jnp.float32)
        back = own[t, 1] + x_recv[t, 1].astype(jnp.float32)
        slopes[t, :, pl.ds(0, hidden)] = (back * gelu_slope(pre)).astype(jnp.bfloat16)
        slope_copy(t).start()

    def project(t):
        slope_copy(t).wait_recv()
        parts[t] = lax.dot_general(
            slopes[t], w1[...], NT_DIMS, preferred_element_type=jnp.float32
        ).astype(jnp.bfloat16)

        @pl.when(t < last)
        def _():
            part_copy(t).start()

        @pl.when(t == last)
        def _():
            part_last().start()

    @pl.loop(0, steps + 2)
    def _(i):
        @pl.when(i < last)
        def _():
            for a in range(2):
                ring(i, a).wait_recv()

                @pl.when(i < last - 1)
                def _():
                    ring(i + 1, a).start()

                @pl.when(i == last - 1)
                def _():
                    ring_last(a).start()

                core_copy(i, a).start()

        @pl.when(i == last)
        def _():
            for a in range(2):
                ring_last(a).wait_recv()
                core_last(a).start()

        @pl.when(i >= 2)
        def _():
            project(i - 2)

        @pl.when((i >= 1) & (i < steps + 1))
        def _():
            bend(i - 1)

        @pl.when(i == 0)
        def _():
            for copy in weights:
                copy.wait()

        @pl.when(i < last)
        def _():
            for a in range(2):
                core_copy(i, a).wait_recv()

        @pl.when(i == last)
        def _():
            for a in range(2):
                core_last(a).wait_recv()

        @pl.when(i < steps)
        def _():
            multiply(i)

    def chunk_of(q):
        where = (1 - core) if q == 0 else core
        return where * share

    def back_copy(t, q):
        chunk = pl.ds(pl.multiple_of(chunk_of(q), share), share)
        return remote(ring_out.at[t, chunk], ring_in.at[t - 1, chunk], back_send.at[t, q], back_recv.at[t, q], behind)

    def back_final(q):
        chunk = pl.ds(pl.multiple_of(chunk_of(q), share), share)
        return remote(ring_out.at[0, chunk], last_in.at[chunk], back_send.at[0, q], back_recv.at[0, q], behind)

    part_last().wait_recv()
    total = parts[last, far].astype(jnp.float32) + cross[last, pl.ds(0, share)].astype(jnp.float32)
    ring_out[last, here] = total.astype(jnp.bfloat16)
    back_copy(last, 1).start()

    @pl.loop(0, last)
    def _(i):
        t = last - 1 - i
        part_copy(t).wait_recv()
        for q in range(2):
            chunk = pl.ds(pl.multiple_of(chunk_of(q), share), share)
            source = pl.ds(pl.multiple_of(core * block + chunk_of(q), share), share)
            if q == 0:
                @pl.when(i > 0)
                def _():
                    back_copy(t + 1, 0).wait_recv()
            else:
                back_copy(t + 1, 1).wait_recv()
            total = parts[t, source].astype(jnp.float32) + cross[t, chunk].astype(jnp.float32)
            ring_out[t, chunk] = (total + ring_in[t, chunk].astype(jnp.float32)).astype(jnp.bfloat16)

            @pl.when(t > 0)
            def _():
                back_copy(t, q).start()

            @pl.when(t == 0)
            def _():
                back_final(q).start()

    there = pl.ds(pl.multiple_of((1 - core) * share, share), share)
    final = remote(last_total, last_cross, last_send.at[0], last_recv.at[0], twin)
    back_final(0).wait_recv()
    last_total[...] = (
        parts[last, there].astype(jnp.float32) + last_in[there].astype(jnp.float32)
    ).astype(jnp.bfloat16)
    final.start()
    back_final(1).wait_recv()
    total = parts[last, here].astype(jnp.float32) + last_in[here].astype(jnp.float32)
    final.wait_recv()
    out_ref[...] = (total + last_cross[...].astype(jnp.float32)).astype(jnp.bfloat16)

    for a in range(2):
        first[a].wait_send()
        ring_first(a).wait_send()
        ring_last(a).wait_send()
        core_last(a).wait_send()
        back_final(a).wait_send()
    part_last().wait_send()
    back_copy(last, 1).wait_send()
    final.wait_send()

    @pl.loop(0, steps)
    def _(t):
        x_copy(t).wait_send()
        slope_copy(t).wait_send()

        @pl.when(t < last)
        def _():
            part_copy(t).wait_send()
            for a in range(2):
                core_copy(t, a).wait_send()

        @pl.when((t > 0) & (t < last))
        def _():
            for a in range(2):
                ring(t, a).wait_send()
                back_copy(t, a).wait_send()


def experts(rows, w_in, w_out):
    levels = lax.axis_size("frm") // 2
    steps = levels // 2
    _, share, half = rows.shape
    block = 2 * share
    hidden = w_in.shape[1]
    bf16 = jnp.bfloat16
    dma = pltpu.SemaphoreType.DMA
    vmem = pl.BlockSpec(memory_space=pltpu.VMEM)
    return pl.pallas_call(
        functools.partial(expert_kernel, levels),
        out_shape=jax.ShapeDtypeStruct((share, half), bf16),
        in_specs=[vmem] * 3,
        out_specs=vmem,
        scratch_shapes=[
            pltpu.VMEM((2, steps, 2 * block, half), bf16),
            pltpu.VMEM((half, 2 * hidden), bf16),
            pltpu.VMEM((2 * hidden, half), bf16),
            pltpu.VMEM((steps, 2, 2 * block, hidden), jnp.float32),
            pltpu.VMEM((steps, 2, 2 * block, hidden), bf16),
            pltpu.VMEM((steps, 2, 2 * block, hidden), bf16),
            pltpu.VMEM((steps, 2 * block, 2 * hidden), bf16),
            pltpu.VMEM((steps, 2 * block, half), bf16),
            pltpu.VMEM((steps, block, half), bf16),
            pltpu.VMEM((steps, block, half), bf16),
            pltpu.VMEM((steps, block, half), bf16),
            pltpu.VMEM((block, half), bf16),
            pltpu.VMEM((share, half), bf16),
            pltpu.VMEM((share, half), bf16),
            dma((4,)), dma((2,)), dma((2,)), dma((2,)), dma((2,)),
            dma((steps, 2)), dma((steps, 2)), dma((steps, 2)), dma((steps, 2)),
            dma((steps,)), dma((steps,)), dma((steps,)), dma((steps,)),
            dma((steps,)), dma((steps,)), dma((steps, 2)), dma((steps, 2)), dma((1,)), dma((1,)),
        ],
        compiler_params=pltpu.CompilerParams(
            collective_id=0, has_side_effects=True, vmem_limit_bytes=48 * 1024 * 1024
        ),
        name="experts",
    )(rows, w_in, w_out)


def body(query_in, key_in, value_in, cotangent, w_in, w_out, gate_probs, chosen):
    frames, blocks, features = query_in.shape
    head_dim = features // HEADS
    scaling = head_dim ** (-0.5)
    groups = lax.axis_size("grp")
    columns = lax.axis_size("frm")
    experts_total = gate_probs.shape[0]
    half = features // 2
    local_rows = frames * blocks
    cot_patch = lax.all_to_all(cotangent, "frm", split_axis=1, concat_axis=0, tiled=True)
    cot_flat = cot_patch.reshape(local_rows, features)
    query_heads = query_in.reshape(frames, blocks, HEADS, head_dim)
    key_heads = key_in.reshape(frames, blocks, HEADS, head_dim)
    value_heads = value_in.reshape(frames, blocks, HEADS, head_dim)
    scores = (
        jnp.einsum("fphd,gphd->phfg", query_heads, key_heads, preferred_element_type=jnp.float32)
        * scaling
    )
    highest = jnp.max(scores, axis=-1, keepdims=True)
    raised = jnp.exp(scores - highest)
    attn_probs = raised / jnp.sum(raised, axis=-1, keepdims=True)
    weights = attn_probs.astype(jnp.bfloat16)
    attn_out = jnp.einsum(
        "phfg,gphd->fphd", weights, value_heads, preferred_element_type=jnp.float32
    )
    attn_out = attn_out.astype(jnp.bfloat16).reshape(local_rows, features)
    patches_all = blocks * groups * columns
    frame_of = chosen // patches_all
    patch_of = chosen % patches_all
    holder = patch_of // blocks
    position = frame_of * blocks + patch_of % blocks
    myself = lax.axis_index("grp") * columns + lax.axis_index("frm")
    owned_here = (holder == myself).astype(jnp.int32)
    ranking = jnp.cumsum(owned_here, axis=1) - 1
    slot_ids = jnp.arange(MOST, dtype=jnp.int32)
    selected = owned_here[:, None, :] * (ranking[:, None, :] == slot_ids[None, :, None]).astype(
        jnp.int32
    )
    position_at = jnp.sum(selected * position[:, None, :], axis=2)
    filled = jnp.sum(selected, axis=2)
    weight_at = jnp.sum(selected.astype(jnp.float32) * gate_probs[:, None, :], axis=2)
    row_ids = jnp.arange(local_rows, dtype=jnp.int32)
    onehot = (
        (position_at[:, :, None] == row_ids[None, None, :]) & (filled[:, :, None] > 0)
    ).astype(jnp.bfloat16)
    picked_in = jnp.einsum(
        "eml,ld->emd", onehot, attn_out, preferred_element_type=jnp.float32
    ).astype(jnp.bfloat16)
    picked_cot = jnp.einsum("eml,ld->emd", onehot, cot_flat, preferred_element_type=jnp.float32)
    scaled = (weight_at[:, :, None] * picked_cot).astype(jnp.bfloat16)
    stacked = jnp.stack([picked_in, scaled], axis=1)
    outgoing = stacked.reshape(experts_total, 2, MOST, 2, half).transpose(0, 3, 1, 2, 4)
    outgoing = outgoing.reshape(groups, 2, MOST, half)
    arrived = lax.all_to_all(outgoing, "grp", split_axis=0, concat_axis=0, tiled=True)
    rows = arrived.transpose(1, 0, 2, 3).reshape(2, groups * MOST, half)
    summed = experts(rows, w_in[0], w_out[0])
    returned = lax.all_to_all(
        summed.reshape(groups, MOST, half), "grp", split_axis=0, concat_axis=0, tiled=True
    )
    flat_back = returned.reshape(experts_total, 2, MOST, half).transpose(0, 2, 1, 3)
    flat_back = flat_back.reshape(experts_total * MOST, features)
    flat_route = onehot.reshape(experts_total * MOST, local_rows)
    added = jnp.einsum("nl,nd->ld", flat_route, flat_back, preferred_element_type=jnp.float32)
    grad_stream = (cot_flat.astype(jnp.float32) + added).astype(jnp.bfloat16)
    grad_heads = grad_stream.reshape(frames, blocks, HEADS, head_dim)
    grad_value = jnp.einsum(
        "phfg,fphd->gphd", weights, grad_heads, preferred_element_type=jnp.float32
    ).astype(jnp.bfloat16)
    grad_prob = jnp.einsum(
        "fphd,gphd->phfg", grad_heads, value_heads, preferred_element_type=jnp.float32
    )
    centre = jnp.sum(attn_probs * grad_prob, axis=-1, keepdims=True)
    grad_score = (attn_probs * (grad_prob - centre)).astype(jnp.bfloat16)
    grad_query = (
        jnp.einsum("phfg,gphd->fphd", grad_score, key_heads, preferred_element_type=jnp.float32)
        * scaling
    ).astype(jnp.bfloat16)
    grad_key = (
        jnp.einsum("phfg,fphd->gphd", grad_score, query_heads, preferred_element_type=jnp.float32)
        * scaling
    ).astype(jnp.bfloat16)
    return (
        grad_query.reshape(frames, blocks, features),
        grad_key.reshape(frames, blocks, features),
        grad_value.reshape(frames, blocks, features),
    )


def solution(mesh):
    return jax.shard_map(
        body,
        mesh=mesh,
        in_specs=(
            P(None, ("grp", "frm"), None),
            P(None, ("grp", "frm"), None),
            P(None, ("grp", "frm"), None),
            P("frm", "grp", None),
            P("grp", None, "frm"),
            P("grp", "frm", None),
            P(),
            P(),
        ),
        out_specs=(
            P(None, ("grp", "frm"), None),
            P(None, ("grp", "frm"), None),
            P(None, ("grp", "frm"), None),
        ),
        check_vma=False,
    )
```

```python
import functools

import jax
import jax.numpy as jnp
from jax import lax
from jax.experimental import pallas as pl
from jax.experimental.pallas import tpu as pltpu
from jax.sharding import PartitionSpec as P

HEADS = 16
MOST = 2
MESH = pl.DeviceIdType.MESH

root_half = 0.7071067811865476
inv_root_tau = 0.3989422804014327


def gelu_slope(pre_act):
    normal_cdf = 0.5 * (1.0 + lax.erf(pre_act * root_half))
    density = jnp.exp(-0.5 * pre_act * pre_act) * inv_root_tau
    return normal_cdf + pre_act * density


NT_DIMS = (((1,), (1,)), ((), ()))
TN_DIMS = (((0,), (0,)), ((), ()))
LAG_MID = 2
LAG_OUT = 3


def bits(n):
    assert n & (n - 1) == 0
    return n.bit_length() - 1


def onehot_rows(chosen, gates, myself, blocks, patches, local_rows):
    experts_total, cap = chosen.shape
    slots = MOST * experts_total

    def twice(values):
        spread = jnp.broadcast_to(values[:, None, :], (experts_total, MOST, cap))
        return spread.reshape(slots, cap)

    token = twice(chosen)
    gate = twice(gates)
    patch = token & (patches - 1)
    frame = lax.shift_right_logical(token, bits(patches))
    holder = lax.shift_right_logical(patch, bits(blocks))
    place = frame * blocks + (patch & (blocks - 1))
    order = lax.broadcasted_iota(jnp.int32, (slots, cap), 1)
    key = (order * local_rows + place).astype(jnp.float32)
    owned = holder == myself
    beyond = float(cap * local_rows)
    low = jnp.min(jnp.where(owned, key, beyond), axis=1, keepdims=True)
    high = jnp.max(jnp.where(owned, key, -1.0), axis=1, keepdims=True)
    odd = (lax.broadcasted_iota(jnp.int32, (slots, 1), 0) & 1) == 1
    key_at = jnp.where(odd, high, low)
    present = jnp.where(odd, (high > low).astype(jnp.float32), (low < beyond).astype(jnp.float32))
    place_at = key_at - jnp.floor(key_at * (1.0 / local_rows)) * local_rows
    gate_at = jnp.sum(jnp.where(owned & (key == key_at), gate, 0.0), axis=1, keepdims=True)
    row = lax.broadcasted_iota(jnp.int32, (slots, local_rows), 1).astype(jnp.float32)
    hit = jnp.where((row == place_at) & (present > 0.5), 1.0, 0.0)
    return hit.astype(jnp.bfloat16), gate_at


def layer_kernel(
    levels, groups, patches,
    query_ref, key_ref, value_ref, cot_ref, w_in_ref, w_out_ref, gates_ref, chosen_ref,
    probs_ref, onehot_ref, stream_ref, back_ref,
    query, key, value, mixed, cot_rows, picked, returned, final_rows,
    gathered, w1, w2, own, x_send, x_recv, slopes, parts, cross, ring_in, ring_out,
    last_in, last_total, last_cross,
    local_sem, load_sem, weight_send, weight_recv, first_send, first_recv,
    ring_send, ring_recv, core_send, core_recv, x_send_sem, x_recv_sem,
    slope_send, slope_recv, part_send, part_recv, back_send, back_recv, last_send, last_recv,
    cot_send, cot_recv, pick_send, pick_recv, return_send, return_recv,
):
    steps = levels // 2
    last = steps - 1
    columns = 2 * levels
    frames, blocks, features = query_ref.shape
    local_rows = frames * blocks
    head_dim = features // HEADS
    half = features // 2
    share = MOST * groups
    block = 2 * share
    hidden = w_in_ref.shape[1]
    grp = lax.axis_index("grp")
    frm = lax.axis_index("frm")
    side = lax.rem(grp, 2)
    expert = lax.div(grp, 2)
    core = lax.rem(frm, 2)
    level = lax.div(frm, 2)
    turn = 1 - 2 * core
    ahead = (grp, lax.rem(level + turn + levels, levels) * 2 + core)
    behind = (grp, lax.rem(level - turn + levels, levels) * 2 + core)
    twin = (grp, frm + turn)
    mate = (grp + 1 - 2 * side, frm)

    def remote(src, dst, send, recv, device):
        return pltpu.make_async_remote_copy(
            src_ref=src, dst_ref=dst, send_sem=send, recv_sem=recv, device_id=device, device_id_type=MESH
        )

    def part_of(index, size):
        return pl.ds(pl.multiple_of(index * size, size), size)

    barrier = pltpu.get_barrier_semaphore()

    @pl.loop(1, columns)
    def _(d):
        pl.semaphore_signal(
            barrier, inc=1, device_id=(grp, lax.rem(frm + d, columns)), device_id_type=MESH
        )

    @pl.loop(1, groups)
    def _(d):
        pl.semaphore_signal(
            barrier, inc=1, device_id=(lax.rem(grp + d, groups), frm), device_id_type=MESH
        )

    mine = part_of(side, half)
    theirs = part_of(1 - side, half)
    here = part_of(core, share)
    lane = part_of(core, block)
    other_lane = part_of(1 - core, block)
    lane_part = pl.ds(pl.multiple_of(core * (block + share), share), share)
    far = pl.ds(pl.multiple_of(block + core * share, share), share)
    other_far = pl.ds(pl.multiple_of(block + (1 - core) * share, share), share)

    inputs = ((query_ref, query), (key_ref, key), (value_ref, value))

    @pl.loop(0, frames)
    def _(f):
        for n, (src, dst) in enumerate(inputs):
            pltpu.make_async_copy(src.at[f], dst.at[part_of(f, blocks)], load_sem.at[n]).start()

    local = [
        pltpu.make_async_copy(w_in_ref.at[mine], w1.at[:, pl.ds(0, hidden)], local_sem.at[0]),
        pltpu.make_async_copy(w_out_ref.at[:, mine], w2.at[pl.ds(0, hidden)], local_sem.at[1]),
        pltpu.make_async_copy(
            cot_ref.at[0, part_of(frm, blocks)], cot_rows.at[part_of(frm, blocks)], local_sem.at[2]
        ),
    ]
    for copy in local:
        copy.start()
    ring_in[last - 1] = jnp.zeros(ring_in.shape[1:], ring_in.dtype)
    myself = grp * columns + frm
    onehot, gate_at = onehot_rows(chosen_ref[...], gates_ref[...], myself, blocks, patches, local_rows)
    onehot_ref[...] = onehot

    pl.semaphore_wait(barrier, columns + groups - 2)

    def cot_copy(other):
        return remote(
            cot_ref.at[0, part_of(other, blocks)], cot_rows.at[part_of(frm, blocks)],
            cot_send.at[other], cot_recv.at[frm], (grp, other),
        )

    def cot_arrival(other):
        return remote(
            cot_ref.at[0, part_of(other, blocks)], cot_rows.at[part_of(other, blocks)],
            cot_send.at[other], cot_recv.at[other], (grp, other),
        )

    @pl.loop(0, levels - 1)
    def _(k):
        away = steps - lax.div(k + 1, 2)
        to = lax.rem(level + levels + (2 * lax.rem(k, 2) - 1) * away, levels)
        cot_copy(2 * to + core).start()
        cot_copy(2 * to + 1 - core).start()

    cot_copy(frm + turn).start()
    weights = [
        remote(w_in_ref.at[theirs], w1.at[:, pl.ds(hidden, hidden)], weight_send.at[0], weight_recv.at[0], mate),
        remote(w_out_ref.at[:, theirs], w2.at[pl.ds(hidden, hidden)], weight_send.at[1], weight_recv.at[1], mate),
    ]
    for copy in weights:
        copy.start()

    for n, (_, dst) in enumerate(inputs):
        pltpu.make_async_copy(dst, dst, load_sem.at[n]).wait()
    row_patch = lax.broadcasted_iota(jnp.int32, (local_rows, local_rows), 0) & (blocks - 1)
    column_patch = lax.broadcasted_iota(jnp.int32, (local_rows, local_rows), 1) & (blocks - 1)
    same = row_patch == column_patch
    scaling = head_dim ** (-0.5)
    together = 4

    @pl.loop(0, HEADS // together)
    def _(n):
        for m in range(together):
            head = n * together + m
            cols = part_of(head, head_dim)
            scores = lax.dot_general(
                query[:, cols], key[:, cols], NT_DIMS, preferred_element_type=jnp.float32
            ) * scaling
            scores = jnp.where(same, scores, -1e30)
            raised = jnp.exp(scores - jnp.max(scores, axis=1, keepdims=True))
            probs = raised / jnp.sum(raised, axis=1, keepdims=True)
            probs_ref[head] = probs
            mixed[:, cols] = jnp.dot(
                probs.astype(jnp.bfloat16), value[:, cols], preferred_element_type=jnp.float32
            ).astype(jnp.bfloat16)

    def pick_copy(a, d):
        to = lax.rem(grp + d, groups)
        return remote(
            picked.at[a, part_of(lax.div(to, 2), MOST), part_of(lax.rem(to, 2), half)],
            gathered.at[a, last, pl.ds(pl.multiple_of(core * share + grp * MOST, MOST), MOST)],
            pick_send.at[a, to], pick_recv.at[a, grp], (to, frm),
        )

    def pick_arrival(a, d):
        to = lax.rem(grp + d, groups)
        return remote(
            picked.at[a, part_of(lax.div(to, 2), MOST), part_of(lax.rem(to, 2), half)],
            gathered.at[a, last, pl.ds(pl.multiple_of(core * share + to * MOST, MOST), MOST)],
            pick_send.at[a, to], pick_recv.at[a, to], (to, frm),
        )

    def pick_own(a):
        return pltpu.make_async_copy(
            picked.at[a, part_of(expert, MOST), part_of(side, half)],
            gathered.at[a, last, pl.ds(pl.multiple_of(core * share + grp * MOST, MOST), MOST)],
            pick_send.at[a, grp],
        )

    def first(a):
        return remote(
            gathered.at[a, last, here], gathered.at[a, last, here], first_send.at[a], first_recv.at[a], twin
        )

    def send_picked(a):
        @pl.loop(1, groups)
        def _(d):
            pick_copy(a, d).start()

        pick_own(a).start()

    def take_picked(a):
        pick_own(a).wait()

        @pl.loop(1, groups)
        def _(d):
            pick_arrival(a, d).wait_recv()

        first(a).start()
        first(a).wait_recv()
        ring_first(a).start()

    picked[0] = jnp.dot(onehot, mixed[...], preferred_element_type=jnp.float32).astype(jnp.bfloat16)
    send_picked(0)

    def ring(t, a):
        return remote(
            gathered.at[a, lax.max(t - 1, 0), lane], gathered.at[a, t, lane], ring_send.at[t, a], ring_recv.at[t, a], ahead
        )

    def ring_first(a):
        return remote(
            gathered.at[a, last, pl.ds(0, block)], gathered.at[a, 0, lane],
            ring_send.at[0, a], ring_recv.at[0, a], ahead,
        )

    def ring_last(a):
        return remote(
            gathered.at[a, last - 1, lane_part], gathered.at[a, last, far],
            ring_send.at[last, a], ring_recv.at[last, a], ahead,
        )

    def core_copy(t, a):
        return remote(
            gathered.at[a, t, lane], gathered.at[a, t, lane], core_send.at[t, a], core_recv.at[t, a], twin
        )

    def core_last(a):
        return remote(
            gathered.at[a, last, far], gathered.at[a, last, far],
            core_send.at[last, a], core_recv.at[last, a], twin,
        )

    def x_copy(t):
        return remote(x_send.at[t], x_recv.at[t], x_send_sem.at[t], x_recv_sem.at[t], mate)

    def slope_copy(t):
        return remote(
            slopes.at[t, :, pl.ds(0, hidden)], slopes.at[t, :, pl.ds(hidden, hidden)],
            slope_send.at[t], slope_recv.at[t], mate,
        )

    def part_copy(t):
        return remote(parts.at[t, other_lane], cross.at[t], part_send.at[t], part_recv.at[t], twin)

    def part_last():
        return remote(
            parts.at[last, other_far], cross.at[last, pl.ds(0, share)],
            part_send.at[last], part_recv.at[last], twin,
        )

    take_picked(0)
    local[2].wait()

    @pl.loop(1, columns)
    def _(d):
        cot_arrival(lax.rem(frm + d, columns)).wait_recv()

    picked_cot = jnp.dot(onehot, cot_rows[...], preferred_element_type=jnp.float32)
    picked[1] = (gate_at * picked_cot).astype(jnp.bfloat16)
    send_picked(1)
    stream_ref[...] = cot_rows[...]
    for copy in local[:2]:
        copy.wait()
    take_picked(1)

    def multiply(t):
        pre = jnp.dot(gathered[0, t], w1[...], preferred_element_type=jnp.float32)
        own[t, 0] = pre[:, :hidden]
        x_send[t, 0] = pre[:, hidden:].astype(jnp.bfloat16)
        back = lax.dot_general(gathered[1, t], w2[...], NT_DIMS, preferred_element_type=jnp.float32)
        own[t, 1] = back[:, :hidden]
        x_send[t, 1] = back[:, hidden:].astype(jnp.bfloat16)
        x_copy(t).start()

    def bend(t):
        x_copy(t).wait_recv()
        pre = own[t, 0] + x_recv[t, 0].astype(jnp.float32)
        back = own[t, 1] + x_recv[t, 1].astype(jnp.float32)
        slopes[t, :, pl.ds(0, hidden)] = (back * gelu_slope(pre)).astype(jnp.bfloat16)
        slope_copy(t).start()

    def project(t):
        slope_copy(t).wait_recv()
        parts[t] = lax.dot_general(
            slopes[t], w1[...], NT_DIMS, preferred_element_type=jnp.float32
        ).astype(jnp.bfloat16)

        @pl.when(t < last)
        def _():
            part_copy(t).start()

        @pl.when(t == last)
        def _():
            part_last().start()

    @pl.loop(0, steps + LAG_OUT)
    def _(i):
        @pl.when(i < last)
        def _():
            for a in range(2):
                ring(i, a).wait_recv()

                @pl.when(i < last - 1)
                def _():
                    ring(i + 1, a).start()

                @pl.when(i == last - 1)
                def _():
                    ring_last(a).start()

                core_copy(i, a).start()

        @pl.when(i == last)
        def _():
            for a in range(2):
                ring_last(a).wait_recv()
                core_last(a).start()

        @pl.when(i >= LAG_OUT)
        def _():
            project(i - LAG_OUT)

        @pl.when((i >= LAG_MID) & (i < steps + LAG_MID))
        def _():
            bend(i - LAG_MID)

        @pl.when(i == 0)
        def _():
            for copy in weights:
                copy.wait_recv()

        @pl.when(i < last)
        def _():
            for a in range(2):
                core_copy(i, a).wait_recv()

        @pl.when(i == last)
        def _():
            for a in range(2):
                core_last(a).wait_recv()

        @pl.when(i < steps)
        def _():
            multiply(i)

    def chunk_of(q):
        where = (1 - core) if q == 0 else core
        return where * share

    def back_copy(t, q):
        chunk = pl.ds(pl.multiple_of(chunk_of(q), share), share)
        return remote(ring_out.at[t, chunk], ring_in.at[t - 1, chunk], back_send.at[t, q], back_recv.at[t, q], behind)

    def back_final(q):
        chunk = pl.ds(pl.multiple_of(chunk_of(q), share), share)
        return remote(ring_out.at[0, chunk], last_in.at[chunk], back_send.at[0, q], back_recv.at[0, q], behind)

    part_last().wait_recv()
    total = parts[last, far].astype(jnp.float32) + cross[last, pl.ds(0, share)].astype(jnp.float32)
    ring_out[last, here] = total.astype(jnp.bfloat16)
    back_copy(last, 1).start()

    @pl.loop(0, last)
    def _(i):
        t = last - 1 - i
        part_copy(t).wait_recv()
        for q in range(2):
            chunk = pl.ds(pl.multiple_of(chunk_of(q), share), share)
            source = pl.ds(pl.multiple_of(core * block + chunk_of(q), share), share)
            if q == 0:
                @pl.when(i > 0)
                def _():
                    back_copy(t + 1, 0).wait_recv()
            else:
                back_copy(t + 1, 1).wait_recv()
            total = parts[t, source].astype(jnp.float32) + cross[t, chunk].astype(jnp.float32)
            ring_out[t, chunk] = (total + ring_in[t, chunk].astype(jnp.float32)).astype(jnp.bfloat16)

            @pl.when(t > 0)
            def _():
                back_copy(t, q).start()

            @pl.when(t == 0)
            def _():
                back_final(q).start()

    there = part_of(1 - core, share)
    final = remote(last_total, last_cross, last_send.at[0], last_recv.at[0], twin)
    back_final(0).wait_recv()
    last_total[...] = (
        parts[last, there].astype(jnp.float32) + last_in[there].astype(jnp.float32)
    ).astype(jnp.bfloat16)
    final.start()
    back_final(1).wait_recv()
    total = parts[last, here].astype(jnp.float32) + last_in[here].astype(jnp.float32)
    final.wait_recv()
    final_rows[...] = (total + last_cross[...].astype(jnp.float32)).astype(jnp.bfloat16)

    def return_copy(d):
        to = lax.rem(grp + d, groups)
        return remote(
            final_rows.at[part_of(to, MOST)], returned.at[part_of(expert, MOST), mine],
            return_send.at[to], return_recv.at[grp], (to, frm),
        )

    def return_arrival(d):
        to = lax.rem(grp + d, groups)
        return remote(
            final_rows.at[part_of(to, MOST)],
            returned.at[part_of(lax.div(to, 2), MOST), part_of(lax.rem(to, 2), half)],
            return_send.at[to], return_recv.at[to], (to, frm),
        )

    return_own = pltpu.make_async_copy(
        final_rows.at[part_of(grp, MOST)], returned.at[part_of(expert, MOST), mine], return_send.at[grp]
    )

    @pl.loop(1, groups)
    def _(d):
        return_copy(d).start()

    return_own.start()

    @pl.loop(1, columns)
    def _(d):
        cot_copy(lax.rem(frm + d, columns)).wait_send()

    @pl.loop(1, groups)
    def _(d):
        for a in range(2):
            pick_copy(a, d).wait_send()

    for a in range(2):
        weights[a].wait_send()
        first(a).wait_send()
        ring_first(a).wait_send()
        ring_last(a).wait_send()
        core_last(a).wait_send()
        back_final(a).wait_send()
    part_last().wait_send()
    back_copy(last, 1).wait_send()
    final.wait_send()

    @pl.loop(0, steps)
    def _(t):
        x_copy(t).wait_send()
        slope_copy(t).wait_send()

        @pl.when(t < last)
        def _():
            part_copy(t).wait_send()
            for a in range(2):
                core_copy(t, a).wait_send()

        @pl.when((t > 0) & (t < last))
        def _():
            for a in range(2):
                ring(t, a).wait_send()
                back_copy(t, a).wait_send()

    return_own.wait()

    @pl.loop(1, groups)
    def _(d):
        return_copy(d).wait_send()
        return_arrival(d).wait_recv()

    back_ref[...] = returned[...]


def layer(query_in, key_in, value_in, cotangent, w_in, w_out, gates, chosen):
    levels = lax.axis_size("frm") // 2
    groups = lax.axis_size("grp")
    frames, blocks, features = query_in.shape
    local_rows = frames * blocks
    steps = levels // 2
    share = MOST * groups
    half = features // 2
    block = 2 * share
    hidden = w_in.shape[1]
    slots = MOST * chosen.shape[0]
    patches = blocks * groups * 2 * levels
    bf16 = jnp.bfloat16
    dma = pltpu.SemaphoreType.DMA
    vmem = pl.BlockSpec(memory_space=pltpu.VMEM)
    hbm = pl.BlockSpec(memory_space=pl.ANY)
    return pl.pallas_call(
        functools.partial(layer_kernel, levels, groups, patches),
        out_shape=(
            jax.ShapeDtypeStruct((HEADS, local_rows, local_rows), jnp.float32),
            jax.ShapeDtypeStruct((slots, local_rows), bf16),
            jax.ShapeDtypeStruct((local_rows, features), bf16),
            jax.ShapeDtypeStruct((slots, features), bf16),
        ),
        in_specs=[hbm] * 6 + [vmem] * 2,
        out_specs=(vmem,) * 4,
        scratch_shapes=[
            pltpu.VMEM((local_rows, features), bf16),
            pltpu.VMEM((local_rows, features), bf16),
            pltpu.VMEM((local_rows, features), bf16),
            pltpu.VMEM((local_rows, features), bf16),
            pltpu.VMEM((local_rows, features), bf16),
            pltpu.VMEM((2, slots, features), bf16),
            pltpu.VMEM((slots, features), bf16),
            pltpu.VMEM((share, half), bf16),
            pltpu.VMEM((2, steps, 2 * block, half), bf16),
            pltpu.VMEM((half, 2 * hidden), bf16),
            pltpu.VMEM((2 * hidden, half), bf16),
            pltpu.VMEM((steps, 2, 2 * block, hidden), jnp.float32),
            pltpu.VMEM((steps, 2, 2 * block, hidden), bf16),
            pltpu.VMEM((steps, 2, 2 * block, hidden), bf16),
            pltpu.VMEM((steps, 2 * block, 2 * hidden), bf16),
            pltpu.VMEM((steps, 2 * block, half), bf16),
            pltpu.VMEM((steps, block, half), bf16),
            pltpu.VMEM((steps, block, half), bf16),
            pltpu.VMEM((steps, block, half), bf16),
            pltpu.VMEM((block, half), bf16),
            pltpu.VMEM((share, half), bf16),
            pltpu.VMEM((share, half), bf16),
            dma((3,)), dma((3,)), dma((2,)), dma((2,)), dma((2,)), dma((2,)),
            dma((steps, 2)), dma((steps, 2)), dma((steps, 2)), dma((steps, 2)),
            dma((steps,)), dma((steps,)), dma((steps,)), dma((steps,)),
            dma((steps,)), dma((steps,)), dma((steps, 2)), dma((steps, 2)), dma((1,)), dma((1,)),
            dma((2 * levels,)), dma((2 * levels,)), dma((2, groups)), dma((2, groups)),
            dma((groups,)), dma((groups,)),
        ],
        compiler_params=pltpu.CompilerParams(
            collective_id=0, has_side_effects=True, vmem_limit_bytes=48 * 1024 * 1024
        ),
        name="layer",
    )(query_in, key_in, value_in, cotangent, w_in, w_out, gates, chosen)


def attention_kernel(
    query_ref, key_ref, value_ref, probs_ref, onehot_ref, stream_ref, back_ref,
    grad_query_ref, grad_key_ref, grad_value_ref,
):
    frames, blocks, width = query_ref.shape
    local_rows = frames * blocks
    heads = probs_ref.shape[0]
    head_dim = width // heads
    scaling = head_dim ** (-0.5)
    added = lax.dot_general(
        onehot_ref[...], back_ref[...], TN_DIMS, preferred_element_type=jnp.float32
    )
    stream = (stream_ref[...].astype(jnp.float32) + added).astype(jnp.bfloat16)
    for n in range(heads):
        cols = slice(n * head_dim, (n + 1) * head_dim)
        grad = stream[:, cols]
        query = query_ref[:, :, cols].reshape(local_rows, head_dim)
        key = key_ref[:, :, cols].reshape(local_rows, head_dim)
        value = value_ref[:, :, cols].reshape(local_rows, head_dim)
        probs = probs_ref[n]
        grad_value = lax.dot_general(
            probs.astype(jnp.bfloat16), grad, TN_DIMS, preferred_element_type=jnp.float32
        )
        grad_value_ref[:, :, cols] = grad_value.astype(jnp.bfloat16).reshape(frames, blocks, head_dim)
        grad_prob = lax.dot_general(grad, value, NT_DIMS, preferred_element_type=jnp.float32)
        centre = jnp.sum(probs * grad_prob, axis=1, keepdims=True)
        grad_score = (probs * (grad_prob - centre)).astype(jnp.bfloat16)
        grad_query = jnp.dot(grad_score, key, preferred_element_type=jnp.float32) * scaling
        grad_query_ref[:, :, cols] = grad_query.astype(jnp.bfloat16).reshape(frames, blocks, head_dim)
        grad_key = lax.dot_general(grad_score, query, TN_DIMS, preferred_element_type=jnp.float32) * scaling
        grad_key_ref[:, :, cols] = grad_key.astype(jnp.bfloat16).reshape(frames, blocks, head_dim)


def attention_back(query_in, key_in, value_in, probs, onehot, stream, back):
    frames, blocks, features = query_in.shape
    local_rows = frames * blocks
    slots = onehot.shape[0]
    pieces = 4
    width = features // pieces
    whole = pl.BlockSpec((frames, blocks, width), lambda n: (0, 0, n))
    return pl.pallas_call(
        attention_kernel,
        grid=(pieces,),
        out_shape=(jax.ShapeDtypeStruct(query_in.shape, jnp.bfloat16),) * 3,
        in_specs=[
            whole, whole, whole,
            pl.BlockSpec((HEADS // pieces, local_rows, local_rows), lambda n: (n, 0, 0)),
            pl.BlockSpec((slots, local_rows), lambda n: (0, 0)),
            pl.BlockSpec((local_rows, width), lambda n: (0, n)),
            pl.BlockSpec((slots, width), lambda n: (0, n)),
        ],
        out_specs=(whole,) * 3,
        compiler_params=pltpu.CompilerParams(dimension_semantics=("arbitrary",)),
        name="attention_back",
    )(query_in, key_in, value_in, probs, onehot, stream, back)


def body(query_in, key_in, value_in, cotangent, w_in, w_out, gate_probs, chosen):
    probs, onehot, stream, back = layer(
        query_in, key_in, value_in, cotangent, w_in[0], w_out[0], gate_probs, chosen
    )
    return attention_back(query_in, key_in, value_in, probs, onehot, stream, back)


def solution(mesh):
    return jax.shard_map(
        body,
        mesh=mesh,
        in_specs=(
            P(None, ("grp", "frm"), None),
            P(None, ("grp", "frm"), None),
            P(None, ("grp", "frm"), None),
            P("frm", "grp", None),
            P("grp", None, "frm"),
            P("grp", "frm", None),
            P(),
            P(),
        ),
        out_specs=(
            P(None, ("grp", "frm"), None),
            P(None, ("grp", "frm"), None),
            P(None, ("grp", "frm"), None),
        ),
        check_vma=False,
    )
```

```python
import functools

import jax
import jax.numpy as jnp
from jax import lax
from jax.experimental import pallas as pl
from jax.experimental.pallas import tpu as pltpu
from jax.sharding import PartitionSpec as P

HEADS = 16
MOST = 2
MESH = pl.DeviceIdType.MESH

root_half = 0.7071067811865476
inv_root_tau = 0.3989422804014327


def gelu_slope(pre_act):
    normal_cdf = 0.5 * (1.0 + lax.erf(pre_act * root_half))
    density = jnp.exp(-0.5 * pre_act * pre_act) * inv_root_tau
    return normal_cdf + pre_act * density


NT_DIMS = (((1,), (1,)), ((), ()))
TN_DIMS = (((0,), (0,)), ((), ()))
LAG_MID = 2
LAG_OUT = 4
LEAD = 1
PIECES = 2
CHUNKS = 4
WIDE = 4


def bits(n):
    assert n & (n - 1) == 0
    return n.bit_length() - 1


def onehot_rows(chosen, gates, myself, blocks, patches, local_rows):
    experts_total, cap = chosen.shape
    slots = MOST * experts_total

    def twice(values):
        spread = jnp.broadcast_to(values[:, None, :], (experts_total, MOST, cap))
        return spread.reshape(slots, cap)

    token = twice(chosen)
    gate = twice(gates)
    patch = token & (patches - 1)
    frame = lax.shift_right_logical(token, bits(patches))
    holder = lax.shift_right_logical(patch, bits(blocks))
    place = frame * blocks + (patch & (blocks - 1))
    order = lax.broadcasted_iota(jnp.int32, (slots, cap), 1)
    key = (order * local_rows + place).astype(jnp.float32)
    owned = holder == myself
    beyond = float(cap * local_rows)
    low = jnp.min(jnp.where(owned, key, beyond), axis=1, keepdims=True)
    high = jnp.max(jnp.where(owned, key, -1.0), axis=1, keepdims=True)
    odd = (lax.broadcasted_iota(jnp.int32, (slots, 1), 0) & 1) == 1
    key_at = jnp.where(odd, high, low)
    present = jnp.where(odd, (high > low).astype(jnp.float32), (low < beyond).astype(jnp.float32))
    place_at = key_at - jnp.floor(key_at * (1.0 / local_rows)) * local_rows
    gate_at = jnp.sum(jnp.where(owned & (key == key_at), gate, 0.0), axis=1, keepdims=True)
    row = lax.broadcasted_iota(jnp.int32, (slots, local_rows), 1).astype(jnp.float32)
    hit = jnp.where((row == place_at) & (present > 0.5), 1.0, 0.0)
    return hit.astype(jnp.bfloat16), gate_at


def layer_kernel(
    levels, groups, patches,
    query_ref, key_ref, value_ref, cot_ref, w_in_ref, w_out_ref, gates_ref, chosen_ref,
    probs_ref, onehot_ref, stream_ref, query_rows_ref, key_rows_ref, value_rows_ref, back_ref,
    query, key, value, mixed, cot_rows, probs_all, onehot_all, picked, returned, final_rows,
    gathered, w1, w2, own, x_send, x_recv, slopes, parts, cross, ring_in, ring_out,
    last_in, gauge,
    local_sem, load_sem, out_sem, own_sem, weight_send, weight_recv,
    ring_send, ring_recv, core_send, core_recv, x_send_sem, x_recv_sem,
    slope_send, slope_recv, part_send, part_recv, back_send, back_recv, last_recv,
    cot_send, cot_recv, pick_send, pick_recv, return_send, return_recv,
):
    steps = levels // 2
    last = steps - 1
    columns = 2 * levels
    frames, blocks, features = query_ref.shape
    local_rows = frames * blocks
    head_dim = features // HEADS
    half = features // 2
    share = MOST * groups
    block = 2 * share
    hidden = w_in_ref.shape[1]
    grp = lax.axis_index("grp")
    frm = lax.axis_index("frm")
    side = lax.rem(grp, 2)
    expert = lax.div(grp, 2)
    core = lax.rem(frm, 2)
    level = lax.div(frm, 2)
    turn = 1 - 2 * core
    ahead = (grp, lax.rem(level + turn + levels, levels) * 2 + core)
    behind = (grp, lax.rem(level - turn + levels, levels) * 2 + core)
    twin = (grp, frm + turn)
    mate = (grp + 1 - 2 * side, frm)

    def remote(src, dst, send, recv, device):
        return pltpu.make_async_remote_copy(
            src_ref=src, dst_ref=dst, send_sem=send, recv_sem=recv, device_id=device, device_id_type=MESH
        )

    def bulk(elements, send, recv):
        lines = elements // (2 * gauge.shape[2])
        many = max(n for n in range(1, gauge.shape[0] + 1) if lines % (8 * n) == 0)
        assert lines * 2 * gauge.shape[2] == elements and lines // many <= gauge.shape[1]
        ref = gauge.at[pl.ds(0, many), pl.ds(0, lines // many)]
        return remote(ref, ref, send, recv, twin)

    def part_of(index, size):
        return pl.ds(pl.multiple_of(index * size, size), size)

    barrier = pltpu.get_barrier_semaphore()

    @pl.loop(1, columns)
    def _(d):
        pl.semaphore_signal(
            barrier, inc=1, device_id=(grp, lax.rem(frm + d, columns)), device_id_type=MESH
        )

    @pl.loop(1, groups)
    def _(d):
        for k in range(2):
            pl.semaphore_signal(
                barrier, inc=1, device_id=(lax.rem(grp + d, groups), frm + k * turn), device_id_type=MESH
            )

    mine = part_of(side, half)
    theirs = part_of(1 - side, half)
    here = part_of(core, share)
    there = part_of(1 - core, share)
    lane = part_of(core, block)
    other_lane = part_of(1 - core, block)
    lane_part = pl.ds(pl.multiple_of(core * (block + share), share), share)
    far = pl.ds(pl.multiple_of(block + core * share, share), share)
    other_far = pl.ds(pl.multiple_of(block + (1 - core) * share, share), share)

    ring_in[last - 1] = jnp.zeros(ring_in.shape[1:], ring_in.dtype)
    pl.semaphore_wait(barrier, columns - 1 + 2 * (groups - 1))

    def cot_copy(other):
        return remote(
            cot_ref.at[0, part_of(other, blocks)], cot_rows.at[part_of(frm, blocks)],
            cot_send.at[0], cot_recv.at[0], (grp, other),
        )

    def cot_all():
        return bulk((columns - 1) * blocks * features, cot_send.at[0], cot_recv.at[0])

    @pl.loop(0, levels - 1)
    def _(k):
        away = steps - lax.div(k + 1, 2)
        to = lax.rem(level + levels + (2 * lax.rem(k, 2) - 1) * away, levels)
        cot_copy(2 * to + core).start()
        cot_copy(2 * to + 1 - core).start()

    cot_copy(frm + turn).start()
    weights = [
        remote(w_in_ref.at[theirs], w1.at[:, pl.ds(hidden, hidden)], weight_send.at[0], weight_recv.at[0], mate),
        remote(w_out_ref.at[:, theirs], w2.at[pl.ds(hidden, hidden)], weight_send.at[0], weight_recv.at[0], mate),
    ]
    for copy in weights:
        copy.start()

    def weights_all():
        return remote(w1, w1, weight_send.at[0], weight_recv.at[0], mate)


    inputs = ((query_ref, query), (key_ref, key), (value_ref, value))

    @pl.loop(0, frames)
    def _(f):
        for n, (src, dst) in enumerate(inputs):
            pltpu.make_async_copy(src.at[f], dst.at[part_of(f, blocks)], load_sem.at[n]).start()

    local = [
        pltpu.make_async_copy(w_in_ref.at[mine], w1.at[:, pl.ds(0, hidden)], local_sem.at[0]),
        pltpu.make_async_copy(w_out_ref.at[:, mine], w2.at[pl.ds(0, hidden)], local_sem.at[1]),
        pltpu.make_async_copy(
            cot_ref.at[0, part_of(frm, blocks)], cot_rows.at[part_of(frm, blocks)], local_sem.at[2]
        ),
    ]
    for copy in local:
        copy.start()
    myself = grp * columns + frm
    onehot, gate_at = onehot_rows(chosen_ref[...], gates_ref[...], myself, blocks, patches, local_rows)
    onehot_all[...] = onehot

    for n, (_, dst) in enumerate(inputs):
        pltpu.make_async_copy(dst, dst, load_sem.at[n]).wait()
    row_patch = lax.broadcasted_iota(jnp.int32, (local_rows, local_rows), 0) & (blocks - 1)
    column_patch = lax.broadcasted_iota(jnp.int32, (local_rows, local_rows), 1) & (blocks - 1)
    same = row_patch == column_patch
    scaling = head_dim ** (-0.5)
    together = 4

    @pl.loop(0, HEADS // together)
    def _(n):
        for m in range(together):
            head = n * together + m
            cols = part_of(head, head_dim)
            scores = lax.dot_general(
                query[:, cols], key[:, cols], NT_DIMS, preferred_element_type=jnp.float32
            ) * scaling
            scores = jnp.where(same, scores, -1e30)
            raised = jnp.exp(scores - jnp.max(scores, axis=1, keepdims=True))
            probs = raised / jnp.sum(raised, axis=1, keepdims=True)
            probs_all[head] = probs
            mixed[:, cols] = jnp.dot(
                probs.astype(jnp.bfloat16), value[:, cols], preferred_element_type=jnp.float32
            ).astype(jnp.bfloat16)

    outs = [
        pltpu.make_async_copy(src, dst, out_sem.at[n])
        for n, (src, dst) in enumerate((
            (probs_all, probs_ref), (onehot_all, onehot_ref), (query, query_rows_ref),
            (key, key_rows_ref), (value, value_rows_ref), (cot_rows, stream_ref),
        ))
    ]

    def pick_copy(a, d, k):
        to = lax.rem(grp + d, groups)
        return remote(
            picked.at[a, part_of(lax.div(to, 2), MOST), part_of(lax.rem(to, 2), half)],
            gathered.at[a, last, pl.ds(pl.multiple_of(core * share + grp * MOST, MOST), MOST)],
            pick_send.at[a], pick_recv.at[a], (to, frm + k * turn),
        )

    def pick_all(a):
        return bulk((block - MOST) * half, pick_send.at[a], pick_recv.at[a])

    def pick_own(a):
        return pltpu.make_async_copy(
            picked.at[a, part_of(expert, MOST), part_of(side, half)],
            gathered.at[a, last, pl.ds(pl.multiple_of(core * share + grp * MOST, MOST), MOST)],
            own_sem.at[a],
        )

    def send_picked(a):
        @pl.loop(1, groups)
        def _(d):
            for k in range(2):
                pick_copy(a, d, k).start()

        pick_copy(a, 0, 1).start()
        pick_own(a).start()

    def take_picked(a):
        pick_own(a).wait()
        pick_all(a).wait_recv()
        for k in range(PIECES):
            ring_first(a, k).start()

    picked[0] = jnp.dot(onehot, mixed[...], preferred_element_type=jnp.float32).astype(jnp.bfloat16)
    send_picked(0)
    for copy in outs[:5]:
        copy.start()

    slab = block // PIECES

    def lane_slab(k):
        return pl.ds(pl.multiple_of(core * block + k * slab, slab), slab)

    def ring(t, a, k):
        return remote(
            gathered.at[a, lax.max(t - 1, 0), lane_slab(k)], gathered.at[a, t, lane_slab(k)],
            ring_send.at[0], ring_recv.at[t, a, k], ahead,
        )

    def ring_first(a, k):
        return remote(
            gathered.at[a, last, pl.ds(k * slab, slab)], gathered.at[a, 0, lane_slab(k)],
            ring_send.at[0], ring_recv.at[0, a, k], ahead,
        )

    def ring_last(a):
        return remote(
            gathered.at[a, last - 1, lane_part], gathered.at[a, last, far],
            ring_send.at[0], ring_recv.at[last, a, 0], ahead,
        )

    def core_copy(t, a, k):
        return remote(
            gathered.at[a, t, lane_slab(k)], gathered.at[a, t, lane_slab(k)],
            core_send.at[0], core_recv.at[t], twin,
        )

    def core_last(a):
        return remote(
            gathered.at[a, last, far], gathered.at[a, last, far],
            core_send.at[0], core_recv.at[last], twin,
        )

    def advance(t, a, k):
        @pl.when(t < last)
        def _():
            ring(t, a, k).wait_recv()

            @pl.when(t < last - 1)
            def _():
                ring(t + 1, a, k).start()

            if k == PIECES - 1:
                @pl.when(t == last - 1)
                def _():
                    ring_last(a).start()

            core_copy(t, a, k).start()

        if k == 0:
            @pl.when(t == last)
            def _():
                ring_last(a).wait_recv()
                core_last(a).start()

    def x_copy(t):
        return remote(x_send.at[t], x_recv.at[t], x_send_sem.at[0], x_recv_sem.at[t], mate)

    def slope_copy(t):
        return remote(
            slopes.at[t, :, pl.ds(0, hidden)], slopes.at[t, :, pl.ds(hidden, hidden)],
            slope_send.at[0], slope_recv.at[t], mate,
        )

    def part_copy(t):
        return remote(parts.at[t, other_lane], cross.at[t], part_send.at[0], part_recv.at[t], twin)

    def part_own():
        return remote(
            parts.at[last, there], cross.at[last, pl.ds(share, share)],
            part_send.at[0], part_recv.at[steps], twin,
        )

    def part_last():
        return remote(
            parts.at[last, other_far], cross.at[last, pl.ds(0, share)],
            part_send.at[0], part_recv.at[last], twin,
        )

    take_picked(0)
    local[2].wait()

    cot_all().wait_recv()

    picked_cot = jnp.dot(onehot_all[...], cot_rows[...], preferred_element_type=jnp.float32)
    picked[1] = (gate_at * picked_cot).astype(jnp.bfloat16)
    send_picked(1)
    for n in range(LEAD):
        for k in range(PIECES):
            advance(jnp.int32(n), 0, k)
    outs[5].start()
    for copy in local[:2]:
        copy.wait()
    take_picked(1)

    def multiply(t):
        pre = jnp.dot(gathered[0, t], w1[...], preferred_element_type=jnp.float32)
        own[t, 0] = pre[:, :hidden]
        x_send[t, 0] = pre[:, hidden:].astype(jnp.bfloat16)
        back = lax.dot_general(gathered[1, t], w2[...], NT_DIMS, preferred_element_type=jnp.float32)
        own[t, 1] = back[:, :hidden]
        x_send[t, 1] = back[:, hidden:].astype(jnp.bfloat16)
        x_copy(t).start()

    def bend(t):
        x_copy(t).wait_recv()
        pre = own[t, 0] + x_recv[t, 0].astype(jnp.float32)
        back = own[t, 1] + x_recv[t, 1].astype(jnp.float32)
        slopes[t, :, pl.ds(0, hidden)] = (back * gelu_slope(pre)).astype(jnp.bfloat16)
        slope_copy(t).start()

    def project(t):
        slope_copy(t).wait_recv()
        parts[t] = lax.dot_general(
            slopes[t], w1[...], NT_DIMS, preferred_element_type=jnp.float32
        ).astype(jnp.bfloat16)

        @pl.when(t < last)
        def _():
            part_copy(t).start()

        @pl.when(t == last)
        def _():
            part_last().start()
            part_own().start()

    @pl.loop(0, steps + LAG_OUT)
    def _(i):
        for k in range(PIECES):
            advance(i, 1, k)
            advance(i + LEAD, 0, k)

        @pl.when((i >= LAG_MID) & (i < steps + LAG_MID))
        def _():
            bend(i - LAG_MID)

        @pl.when(i >= LAG_OUT)
        def _():
            project(i - LAG_OUT)

        @pl.when(i == 0)
        def _():
            weights_all().wait_recv()

        @pl.when(i < last)
        def _():
            whole = gathered.at[:, i, other_lane]
            remote(whole, whole, core_send.at[0], core_recv.at[i], twin).wait_recv()

        @pl.when(i == last)
        def _():
            whole = gathered.at[:, last, other_far]
            remote(whole, whole, core_send.at[0], core_recv.at[last], twin).wait_recv()

        @pl.when(i < steps)
        def _():
            multiply(i)

    piece = block // CHUNKS

    def chunk_of(q):
        where = (1 - core) if q < CHUNKS // 2 else core
        return where * share + (q % (CHUNKS // 2)) * piece

    def back_copy(t, q):
        chunk = pl.ds(pl.multiple_of(chunk_of(q), piece), piece)
        return remote(
            ring_out.at[t, chunk], ring_in.at[lax.max(t - 1, 0), chunk], back_send.at[0], back_recv.at[t, q], behind
        )

    def back_final(q):
        chunk = pl.ds(pl.multiple_of(chunk_of(q), piece), piece)
        n = q % (CHUNKS // 2)
        owner = (1 - core) if q < CHUNKS // 2 else core
        return remote(
            ring_out.at[0, chunk], last_in.at[core, pl.ds(n * piece, piece)],
            back_send.at[0], last_recv.at[core, n], (grp, behind[1] - core + owner),
        )

    def back_arrival(way, n):
        return remote(
            ring_out.at[0, pl.ds(0, piece)], last_in.at[way, pl.ds(n * piece, piece)],
            back_send.at[0], last_recv.at[way, n], ahead,
        )

    part_last().wait_recv()
    for q in range(CHUNKS // 2, CHUNKS):
        chunk = pl.ds(pl.multiple_of(chunk_of(q), piece), piece)
        source = pl.ds(pl.multiple_of(block + chunk_of(q), piece), piece)
        other = pl.ds((q - CHUNKS // 2) * piece, piece)
        total = parts[last, source].astype(jnp.float32) + cross[last, other].astype(jnp.float32)
        ring_out[last, chunk] = total.astype(jnp.bfloat16)
        back_copy(last, q).start()

    @pl.loop(0, last)
    def _(i):
        t = last - 1 - i
        part_copy(t).wait_recv()
        for q in range(CHUNKS):
            chunk = pl.ds(pl.multiple_of(chunk_of(q), piece), piece)
            source = pl.ds(pl.multiple_of(core * block + chunk_of(q), piece), piece)
            total = parts[t, source].astype(jnp.float32) + cross[t, chunk].astype(jnp.float32)
            if q < CHUNKS // 2:
                @pl.when(i > 0)
                def _():
                    back_copy(t + 1, q).wait_recv()
            else:
                back_copy(t + 1, q).wait_recv()
            ring_out[t, chunk] = (total + ring_in[t, chunk].astype(jnp.float32)).astype(jnp.bfloat16)

            @pl.when(t > 0)
            def _():
                back_copy(t, q).start()

            @pl.when(t == 0)
            def _():
                back_final(q).start()

    def return_copy(to):
        return remote(
            final_rows.at[part_of(to, MOST)], returned.at[part_of(expert, MOST), mine],
            return_send.at[0], return_recv.at[0], (to, frm),
        )

    def return_all():
        return bulk((share - MOST) * half, return_send.at[0], return_recv.at[0])

    return_own = pltpu.make_async_copy(
        final_rows.at[part_of(grp, MOST)], returned.at[part_of(expert, MOST), mine], own_sem.at[2]
    )
    part_own().wait_recv()
    reach = piece // MOST
    for n in range(CHUNKS // 2):
        rows = pl.ds(pl.multiple_of(core * share + n * piece, piece), piece)
        other = pl.ds(share + n * piece, piece)
        chunk = pl.ds(n * piece, piece)
        total = parts[last, rows].astype(jnp.float32) + cross[last, other].astype(jnp.float32)
        for way in range(2):
            back_arrival(way, n).wait_recv()
        total = total + last_in[0, chunk].astype(jnp.float32) + last_in[1, chunk].astype(jnp.float32)
        final_rows[chunk] = total.astype(jnp.bfloat16)

        @pl.loop(0, reach)
        def _(j):
            to = n * reach + lax.rem(grp + j, reach)

            @pl.when(to != grp)
            def _():
                return_copy(to).start()

            @pl.when(to == grp)
            def _():
                return_own.start()

    cot_all().wait_send()

    for copy in outs:
        copy.wait()

    for a in range(2):
        pick_all(a).wait_send()
    weights_all().wait_send()
    moved = (last * block + share) * half
    bulk(2 * moved, ring_send.at[0], ring_recv.at[0, 0, 0]).wait_send()
    bulk(2 * moved, core_send.at[0], core_recv.at[0]).wait_send()
    remote(cross, cross, part_send.at[0], part_recv.at[0], twin).wait_send()
    remote(x_send, x_recv, x_send_sem.at[0], x_recv_sem.at[0], mate).wait_send()
    slopes_all = slopes.at[:, :, pl.ds(0, hidden)]
    remote(slopes_all, slopes_all, slope_send.at[0], slope_recv.at[0], mate).wait_send()
    bulk(moved, back_send.at[0], back_recv.at[0, 0]).wait_send()
    return_own.wait()

    return_all().wait_send()
    return_all().wait_recv()
    back_ref[...] = returned[...]


def layer(query_in, key_in, value_in, cotangent, w_in, w_out, gates, chosen):
    levels = lax.axis_size("frm") // 2
    groups = lax.axis_size("grp")
    frames, blocks, features = query_in.shape
    local_rows = frames * blocks
    steps = levels // 2
    share = MOST * groups
    half = features // 2
    block = 2 * share
    hidden = w_in.shape[1]
    slots = MOST * chosen.shape[0]
    patches = blocks * groups * 2 * levels
    bf16 = jnp.bfloat16
    dma = pltpu.SemaphoreType.DMA
    vmem = pl.BlockSpec(memory_space=pltpu.VMEM)
    hbm = pl.BlockSpec(memory_space=pl.ANY)
    return pl.pallas_call(
        functools.partial(layer_kernel, levels, groups, patches),
        out_shape=(
            jax.ShapeDtypeStruct((HEADS, local_rows, local_rows), jnp.float32),
            jax.ShapeDtypeStruct((slots, local_rows), bf16),
            jax.ShapeDtypeStruct((local_rows, features), bf16),
            jax.ShapeDtypeStruct((local_rows, features), bf16),
            jax.ShapeDtypeStruct((local_rows, features), bf16),
            jax.ShapeDtypeStruct((local_rows, features), bf16),
            jax.ShapeDtypeStruct((slots, features), bf16),
        ),
        in_specs=[hbm] * 6 + [vmem] * 2,
        out_specs=(hbm,) * 6 + (vmem,),
        scratch_shapes=[
            pltpu.VMEM((local_rows, features), bf16),
            pltpu.VMEM((local_rows, features), bf16),
            pltpu.VMEM((local_rows, features), bf16),
            pltpu.VMEM((local_rows, features), bf16),
            pltpu.VMEM((local_rows, features), bf16),
            pltpu.VMEM((HEADS, local_rows, local_rows), jnp.float32),
            pltpu.VMEM((slots, local_rows), bf16),
            pltpu.VMEM((2, slots, features), bf16),
            pltpu.VMEM((slots, features), bf16),
            pltpu.VMEM((share, half), bf16),
            pltpu.VMEM((2, steps, 2 * block, half), bf16),
            pltpu.VMEM((half, 2 * hidden), bf16),
            pltpu.VMEM((2 * hidden, half), bf16),
            pltpu.VMEM((steps, 2, 2 * block, hidden), jnp.float32),
            pltpu.VMEM((steps, 2, 2 * block, hidden), bf16),
            pltpu.VMEM((steps, 2, 2 * block, hidden), bf16),
            pltpu.VMEM((steps, 2 * block, 2 * hidden), bf16),
            pltpu.VMEM((steps, 2 * block, half), bf16),
            pltpu.VMEM((steps, block, half), bf16),
            pltpu.VMEM((steps, block, half), bf16),
            pltpu.VMEM((steps, block, half), bf16),
            pltpu.VMEM((2, share, half), bf16),
            pltpu.VMEM((32, 128, 128), jnp.float32),
            dma((3,)), dma((3,)), dma((6,)), dma((3,)), dma((1,)), dma((1,)),
            dma((1,)), dma((steps, 2, PIECES)), dma((1,)), dma((steps,)),
            dma((1,)), dma((steps,)), dma((1,)), dma((steps,)),
            dma((1,)), dma((steps + 1,)), dma((1,)), dma((steps, CHUNKS)), dma((2, CHUNKS // 2)),
            dma((1,)), dma((1,)), dma((2,)), dma((2,)), dma((1,)), dma((1,)),
        ],
        compiler_params=pltpu.CompilerParams(
            collective_id=0, has_side_effects=True
        ),
        name="layer",
    )(query_in, key_in, value_in, cotangent, w_in, w_out, gates, chosen)


def attention_kernel(
    query_ref, key_ref, value_ref, probs_ref, onehot_ref, stream_ref, back_ref,
    grad_query_ref, grad_key_ref, grad_value_ref,
):
    frames, blocks, width = grad_query_ref.shape
    local_rows = frames * blocks
    heads = probs_ref.shape[0]
    head_dim = width // heads
    scaling = head_dim ** (-0.5)
    added = lax.dot_general(
        onehot_ref[...], back_ref[...], TN_DIMS, preferred_element_type=jnp.float32
    )
    stream = (stream_ref[...].astype(jnp.float32) + added).astype(jnp.bfloat16)
    for n in range(heads):
        cols = slice(n * head_dim, (n + 1) * head_dim)
        grad = stream[:, cols]
        query = query_ref[:, cols]
        key = key_ref[:, cols]
        value = value_ref[:, cols]
        probs = probs_ref[n]
        grad_value = lax.dot_general(
            probs.astype(jnp.bfloat16), grad, TN_DIMS, preferred_element_type=jnp.float32
        )
        grad_value_ref[:, :, cols] = grad_value.astype(jnp.bfloat16).reshape(frames, blocks, head_dim)
        grad_prob = lax.dot_general(grad, value, NT_DIMS, preferred_element_type=jnp.float32)
        centre = jnp.sum(probs * grad_prob, axis=1, keepdims=True)
        grad_score = (probs * (grad_prob - centre)).astype(jnp.bfloat16)
        grad_query = jnp.dot(grad_score, key, preferred_element_type=jnp.float32) * scaling
        grad_query_ref[:, :, cols] = grad_query.astype(jnp.bfloat16).reshape(frames, blocks, head_dim)
        grad_key = lax.dot_general(grad_score, query, TN_DIMS, preferred_element_type=jnp.float32) * scaling
        grad_key_ref[:, :, cols] = grad_key.astype(jnp.bfloat16).reshape(frames, blocks, head_dim)


def attention_back(frames, query, key, value, probs, onehot, stream, back):
    local_rows, features = query.shape
    blocks = local_rows // frames
    slots = onehot.shape[0]
    width = features // WIDE
    rows = pl.BlockSpec((local_rows, width), lambda n: (0, n))
    whole = pl.BlockSpec((frames, blocks, width), lambda n: (0, 0, n))
    return pl.pallas_call(
        attention_kernel,
        grid=(WIDE,),
        out_shape=(jax.ShapeDtypeStruct((frames, blocks, features), jnp.bfloat16),) * 3,
        in_specs=[
            rows, rows, rows,
            pl.BlockSpec((HEADS // WIDE, local_rows, local_rows), lambda n: (n, 0, 0)),
            pl.BlockSpec((slots, local_rows), lambda n: (0, 0)),
            rows,
            pl.BlockSpec((slots, width), lambda n: (0, n)),
        ],
        out_specs=(whole,) * 3,
        compiler_params=pltpu.CompilerParams(dimension_semantics=("arbitrary",)),
        name="attention_back",
    )(query, key, value, probs, onehot, stream, back)


def body(query_in, key_in, value_in, cotangent, w_in, w_out, gate_probs, chosen):
    probs, onehot, stream, query, key, value, back = layer(
        query_in, key_in, value_in, cotangent, w_in[0], w_out[0], gate_probs, chosen
    )
    return attention_back(query_in.shape[0], query, key, value, probs, onehot, stream, back)


def solution(mesh):
    return jax.shard_map(
        body,
        mesh=mesh,
        in_specs=(
            P(None, ("grp", "frm"), None),
            P(None, ("grp", "frm"), None),
            P(None, ("grp", "frm"), None),
            P("frm", "grp", None),
            P("grp", None, "frm"),
            P("grp", "frm", None),
            P(),
            P(),
        ),
        out_specs=(
            P(None, ("grp", "frm"), None),
            P(None, ("grp", "frm"), None),
            P(None, ("grp", "frm"), None),
        ),
        check_vma=False,
    )
```

```python
import functools

import jax
import jax.numpy as jnp
from jax import lax
from jax.experimental import pallas as pl
from jax.experimental.pallas import tpu as pltpu
from jax.sharding import PartitionSpec as P

HEADS = 16
MOST = 2
MESH = pl.DeviceIdType.MESH

root_half = 0.7071067811865476
inv_root_tau = 0.3989422804014327


def gelu_slope(pre_act):
    normal_cdf = 0.5 * (1.0 + lax.erf(pre_act * root_half))
    density = jnp.exp(-0.5 * pre_act * pre_act) * inv_root_tau
    return normal_cdf + pre_act * density


NT_DIMS = (((1,), (1,)), ((), ()))
TN_DIMS = (((0,), (0,)), ((), ()))
LAG_MID = 2
LAG_OUT = 4
LEAD = 1
PIECES = 2
CHUNKS = 4
WIDE = 4
EARLY = 2


def bits(n):
    assert n & (n - 1) == 0
    return n.bit_length() - 1


def onehot_rows(chosen, gates, myself, blocks, patches, local_rows):
    experts_total, cap = chosen.shape
    slots = MOST * experts_total

    def twice(values):
        spread = jnp.broadcast_to(values[:, None, :], (experts_total, MOST, cap))
        return spread.reshape(slots, cap)

    token = twice(chosen)
    gate = twice(gates)
    patch = token & (patches - 1)
    frame = lax.shift_right_logical(token, bits(patches))
    holder = lax.shift_right_logical(patch, bits(blocks))
    place = frame * blocks + (patch & (blocks - 1))
    order = lax.broadcasted_iota(jnp.int32, (slots, cap), 1)
    key = (order * local_rows + place).astype(jnp.float32)
    owned = holder == myself
    beyond = float(cap * local_rows)
    low = jnp.min(jnp.where(owned, key, beyond), axis=1, keepdims=True)
    high = jnp.max(jnp.where(owned, key, -1.0), axis=1, keepdims=True)
    odd = (lax.broadcasted_iota(jnp.int32, (slots, 1), 0) & 1) == 1
    key_at = jnp.where(odd, high, low)
    present = jnp.where(odd, (high > low).astype(jnp.float32), (low < beyond).astype(jnp.float32))
    place_at = key_at - jnp.floor(key_at * (1.0 / local_rows)) * local_rows
    gate_at = jnp.sum(jnp.where(owned & (key == key_at), gate, 0.0), axis=1, keepdims=True)
    row = lax.broadcasted_iota(jnp.int32, (slots, local_rows), 1).astype(jnp.float32)
    hit = jnp.where((row == place_at) & (present > 0.5), 1.0, 0.0)
    return hit.astype(jnp.bfloat16), gate_at


def layer_kernel(
    levels, groups, patches,
    query_ref, key_ref, value_ref, cot_ref, w_in_ref, w_out_ref, gates_ref, chosen_ref,
    probs_ref, onehot_ref, stream_ref, query_rows_ref, key_rows_ref, value_rows_ref, back_ref,
    query, key, value, mixed, cot_rows, probs_all, onehot_all, picked, returned, final_rows,
    gathered, w1, w2, own, x_send, x_recv, slopes, parts, cross, ring_in, ring_out,
    last_in, far_in, gauge,
    local_sem, load_sem, out_sem, own_sem, weight_send, weight_recv,
    ring_send, ring_recv, core_send, core_recv, x_send_sem, x_recv_sem,
    slope_send, slope_recv, part_send, part_recv, back_send, back_recv, last_recv, jump_recv,
    cot_send, cot_recv, pick_send, pick_recv, return_send, return_recv,
):
    steps = levels // 2
    last = steps - 1
    near = steps * 5 // 8
    columns = 2 * levels
    frames, blocks, features = query_ref.shape
    local_rows = frames * blocks
    head_dim = features // HEADS
    half = features // 2
    share = MOST * groups
    block = 2 * share
    hidden = w_in_ref.shape[1]
    grp = lax.axis_index("grp")
    frm = lax.axis_index("frm")
    side = lax.rem(grp, 2)
    expert = lax.div(grp, 2)
    core = lax.rem(frm, 2)
    level = lax.div(frm, 2)
    turn = 1 - 2 * core
    ahead = (grp, lax.rem(level + turn + levels, levels) * 2 + core)
    behind = (grp, lax.rem(level - turn + levels, levels) * 2 + core)
    twin = (grp, frm + turn)
    mate = (grp + 1 - 2 * side, frm)

    def remote(src, dst, send, recv, device):
        return pltpu.make_async_remote_copy(
            src_ref=src, dst_ref=dst, send_sem=send, recv_sem=recv, device_id=device, device_id_type=MESH
        )

    def bulk(elements, send, recv):
        lines = elements // (2 * gauge.shape[2])
        many = max(n for n in range(1, gauge.shape[0] + 1) if lines % (8 * n) == 0)
        assert lines * 2 * gauge.shape[2] == elements and lines // many <= gauge.shape[1]
        ref = gauge.at[pl.ds(0, many), pl.ds(0, lines // many)]
        return remote(ref, ref, send, recv, twin)

    def part_of(index, size):
        return pl.ds(pl.multiple_of(index * size, size), size)

    barrier = pltpu.get_barrier_semaphore()

    @pl.loop(1, columns)
    def _(d):
        pl.semaphore_signal(
            barrier, inc=1, device_id=(grp, lax.rem(frm + d, columns)), device_id_type=MESH
        )

    @pl.loop(1, groups)
    def _(d):
        for k in range(2):
            pl.semaphore_signal(
                barrier, inc=1, device_id=(lax.rem(grp + d, groups), frm + k * turn), device_id_type=MESH
            )

    mine = part_of(side, half)
    theirs = part_of(1 - side, half)
    here = part_of(core, share)
    there = part_of(1 - core, share)
    lane = part_of(core, block)
    other_lane = part_of(1 - core, block)
    lane_part = pl.ds(pl.multiple_of(core * (block + share), share), share)
    far = pl.ds(pl.multiple_of(block + core * share, share), share)
    other_far = pl.ds(pl.multiple_of(block + (1 - core) * share, share), share)

    pl.semaphore_wait(barrier, columns - 1 + 2 * (groups - 1))

    def cot_copy(other):
        return remote(
            cot_ref.at[0, part_of(other, blocks)], cot_rows.at[part_of(frm, blocks)],
            cot_send.at[0], cot_recv.at[0], (grp, other),
        )

    def cot_all():
        return bulk((columns - 1) * blocks * features, cot_send.at[0], cot_recv.at[0])

    @pl.loop(0, levels - 1)
    def _(k):
        away = steps - lax.div(k + 1, 2)
        to = lax.rem(level + levels + (2 * lax.rem(k, 2) - 1) * away, levels)
        cot_copy(2 * to + core).start()
        cot_copy(2 * to + 1 - core).start()

    cot_copy(frm + turn).start()
    weights = [
        remote(w_in_ref.at[theirs], w1.at[:, pl.ds(hidden, hidden)], weight_send.at[0], weight_recv.at[0], mate),
        remote(w_out_ref.at[:, theirs], w2.at[pl.ds(hidden, hidden)], weight_send.at[0], weight_recv.at[0], mate),
    ]
    for copy in weights:
        copy.start()

    def weights_all():
        return remote(w1, w1, weight_send.at[0], weight_recv.at[0], mate)


    inputs = ((query_ref, query), (key_ref, key), (value_ref, value))

    @pl.loop(0, frames)
    def _(f):
        for n, (src, dst) in enumerate(inputs):
            pltpu.make_async_copy(src.at[f], dst.at[part_of(f, blocks)], load_sem.at[n]).start()

    local = [
        pltpu.make_async_copy(w_in_ref.at[mine], w1.at[:, pl.ds(0, hidden)], local_sem.at[0]),
        pltpu.make_async_copy(w_out_ref.at[:, mine], w2.at[pl.ds(0, hidden)], local_sem.at[1]),
        pltpu.make_async_copy(
            cot_ref.at[0, part_of(frm, blocks)], cot_rows.at[part_of(frm, blocks)], local_sem.at[2]
        ),
    ]
    for copy in local:
        copy.start()
    myself = grp * columns + frm
    onehot, gate_at = onehot_rows(chosen_ref[...], gates_ref[...], myself, blocks, patches, local_rows)
    onehot_all[...] = onehot

    for n, (_, dst) in enumerate(inputs):
        pltpu.make_async_copy(dst, dst, load_sem.at[n]).wait()
    row_patch = lax.broadcasted_iota(jnp.int32, (local_rows, local_rows), 0) & (blocks - 1)
    column_patch = lax.broadcasted_iota(jnp.int32, (local_rows, local_rows), 1) & (blocks - 1)
    same = row_patch == column_patch
    scaling = head_dim ** (-0.5)
    together = 4

    @pl.loop(0, HEADS // together)
    def _(n):
        for m in range(together):
            head = n * together + m
            cols = part_of(head, head_dim)
            scores = lax.dot_general(
                query[:, cols], key[:, cols], NT_DIMS, preferred_element_type=jnp.float32
            ) * scaling
            scores = jnp.where(same, scores, -1e30)
            raised = jnp.exp(scores - jnp.max(scores, axis=1, keepdims=True))
            probs = raised / jnp.sum(raised, axis=1, keepdims=True)
            probs_all[head] = probs
            mixed[:, cols] = jnp.dot(
                probs.astype(jnp.bfloat16), value[:, cols], preferred_element_type=jnp.float32
            ).astype(jnp.bfloat16)

    outs = [
        pltpu.make_async_copy(src, dst, out_sem.at[n])
        for n, (src, dst) in enumerate((
            (probs_all, probs_ref), (onehot_all, onehot_ref), (query, query_rows_ref),
            (key, key_rows_ref), (value, value_rows_ref), (cot_rows, stream_ref),
        ))
    ]

    def pick_copy(a, d, k):
        to = lax.rem(grp + d, groups)
        return remote(
            picked.at[a, part_of(lax.div(to, 2), MOST), part_of(lax.rem(to, 2), half)],
            gathered.at[a, last, pl.ds(pl.multiple_of(core * share + grp * MOST, MOST), MOST)],
            pick_send.at[a], pick_recv.at[a], (to, frm + k * turn),
        )

    def pick_all(a):
        return bulk((block - MOST) * half, pick_send.at[a], pick_recv.at[a])

    def pick_own(a):
        return pltpu.make_async_copy(
            picked.at[a, part_of(expert, MOST), part_of(side, half)],
            gathered.at[a, last, pl.ds(pl.multiple_of(core * share + grp * MOST, MOST), MOST)],
            own_sem.at[a],
        )

    def send_picked(a):
        @pl.loop(1, groups)
        def _(d):
            for k in range(2):
                pick_copy(a, d, k).start()

        pick_copy(a, 0, 1).start()
        pick_own(a).start()

    def take_picked(a):
        pick_own(a).wait()
        pick_all(a).wait_recv()
        for k in range(PIECES):
            ring_first(a, k).start()

    picked[0] = jnp.dot(onehot, mixed[...], preferred_element_type=jnp.float32).astype(jnp.bfloat16)
    send_picked(0)
    for copy in outs[:5]:
        copy.start()

    slab = block // PIECES

    def lane_slab(k):
        return pl.ds(pl.multiple_of(core * block + k * slab, slab), slab)

    def ring(t, a, k):
        return remote(
            gathered.at[a, lax.max(t - 1, 0), lane_slab(k)], gathered.at[a, t, lane_slab(k)],
            ring_send.at[0], ring_recv.at[t, a, k], ahead,
        )

    def ring_first(a, k):
        return remote(
            gathered.at[a, last, pl.ds(k * slab, slab)], gathered.at[a, 0, lane_slab(k)],
            ring_send.at[0], ring_recv.at[0, a, k], ahead,
        )

    def ring_last(a):
        return remote(
            gathered.at[a, last - 1, lane_part], gathered.at[a, last, far],
            ring_send.at[0], ring_recv.at[last, a, 0], ahead,
        )

    def core_copy(t, a, k):
        return remote(
            gathered.at[a, t, lane_slab(k)], gathered.at[a, t, lane_slab(k)],
            core_send.at[0], core_recv.at[t], twin,
        )

    def core_last(a):
        return remote(
            gathered.at[a, last, far], gathered.at[a, last, far],
            core_send.at[0], core_recv.at[last], twin,
        )

    def advance(t, a, k):
        @pl.when(t < last)
        def _():
            ring(t, a, k).wait_recv()

            @pl.when(t < last - 1)
            def _():
                ring(t + 1, a, k).start()

            if k == PIECES - 1:
                @pl.when(t == last - 1)
                def _():
                    ring_last(a).start()

            core_copy(t, a, k).start()

        if k == 0:
            @pl.when(t == last)
            def _():
                ring_last(a).wait_recv()
                core_last(a).start()

    def x_copy(t):
        return remote(x_send.at[t], x_recv.at[t], x_send_sem.at[0], x_recv_sem.at[t], mate)

    def slope_copy(t):
        return remote(
            slopes.at[t, :, pl.ds(0, hidden)], slopes.at[t, :, pl.ds(hidden, hidden)],
            slope_send.at[0], slope_recv.at[t], mate,
        )

    def part_copy(t):
        return remote(parts.at[t, other_lane], cross.at[t], part_send.at[0], part_recv.at[t], twin)

    def part_own():
        return remote(
            parts.at[last, there], cross.at[last, pl.ds(share, share)],
            part_send.at[0], part_recv.at[steps], twin,
        )

    def part_last():
        return remote(
            parts.at[last, other_far], cross.at[last, pl.ds(0, share)],
            part_send.at[0], part_recv.at[last], twin,
        )

    take_picked(0)
    local[2].wait()

    cot_all().wait_recv()

    picked_cot = jnp.dot(onehot_all[...], cot_rows[...], preferred_element_type=jnp.float32)
    picked[1] = (gate_at * picked_cot).astype(jnp.bfloat16)
    send_picked(1)
    for n in range(LEAD):
        for k in range(PIECES):
            advance(jnp.int32(n), 0, k)
    outs[5].start()
    for copy in local[:2]:
        copy.wait()
    take_picked(1)

    def multiply(t):
        pre = jnp.dot(gathered[0, t], w1[...], preferred_element_type=jnp.float32)
        own[t, 0] = pre[:, :hidden]
        x_send[t, 0] = pre[:, hidden:].astype(jnp.bfloat16)
        back = lax.dot_general(gathered[1, t], w2[...], NT_DIMS, preferred_element_type=jnp.float32)
        own[t, 1] = back[:, :hidden]
        x_send[t, 1] = back[:, hidden:].astype(jnp.bfloat16)
        x_copy(t).start()

    def bend(t):
        x_copy(t).wait_recv()
        pre = own[t, 0] + x_recv[t, 0].astype(jnp.float32)
        back = own[t, 1] + x_recv[t, 1].astype(jnp.float32)
        slopes[t, :, pl.ds(0, hidden)] = (back * gelu_slope(pre)).astype(jnp.bfloat16)
        slope_copy(t).start()

    def project(t):
        slope_copy(t).wait_recv()
        parts[t] = lax.dot_general(
            slopes[t], w1[...], NT_DIMS, preferred_element_type=jnp.float32
        ).astype(jnp.bfloat16)

        @pl.when(t < last)
        def _():
            part_copy(t).start()

        @pl.when(t == last)
        def _():
            part_last().start()
            part_own().start()

    piece = block // CHUNKS

    def chunk_of(q):
        where = (1 - core) if q < CHUNKS // 2 else core
        return where * share + (q % (CHUNKS // 2)) * piece

    def back_copy(t, q):
        chunk = pl.ds(pl.multiple_of(chunk_of(q), piece), piece)
        return remote(
            ring_out.at[t, chunk], ring_in.at[t - 1, chunk], back_send.at[0], back_recv.at[t, q], behind
        )

    def back_final(q):
        chunk = pl.ds(pl.multiple_of(chunk_of(q), piece), piece)
        n = q % (CHUNKS // 2)
        owner = (1 - core) if q < CHUNKS // 2 else core
        return remote(
            ring_out.at[0, chunk], last_in.at[core, pl.ds(n * piece, piece)],
            back_send.at[0], last_recv.at[core, n], (grp, behind[1] - core + owner),
        )

    def jump(q):
        chunk = pl.ds(pl.multiple_of(chunk_of(q), piece), piece)
        n = q % (CHUNKS // 2)
        owner = (1 - core) if q < CHUNKS // 2 else core
        home = lax.rem(level + levels - turn * (near + 1), levels)
        return remote(
            ring_out.at[near, chunk], far_in.at[core, pl.ds(n * piece, piece)],
            back_send.at[0], jump_recv.at[core, n], (grp, 2 * home + owner),
        )

    def arrival(buffer, sem, way, n):
        ref = buffer.at[way, pl.ds(n * piece, piece)]
        return remote(ref, ref, back_send.at[0], sem.at[way, n], twin)

    def scatter_first():
        part_last().wait_recv()
        for q in range(CHUNKS // 2, CHUNKS):
            chunk = pl.ds(pl.multiple_of(chunk_of(q), piece), piece)
            source = pl.ds(pl.multiple_of(block + chunk_of(q), piece), piece)
            other = pl.ds((q - CHUNKS // 2) * piece, piece)
            total = parts[last, source].astype(jnp.float32) + cross[last, other].astype(jnp.float32)
            ring_out[last, chunk] = total.astype(jnp.bfloat16)
            back_copy(last, q).start()

    def scatter(t):
        part_copy(t).wait_recv()
        for q in range(CHUNKS):
            chunk = pl.ds(pl.multiple_of(chunk_of(q), piece), piece)
            source = pl.ds(pl.multiple_of(core * block + chunk_of(q), piece), piece)
            total = parts[t, source].astype(jnp.float32) + cross[t, chunk].astype(jnp.float32)
            begun = t == near - 1 or (t == last - 1 and q < CHUNKS // 2)
            if not begun:
                back_copy(t + 1, q).wait_recv()
                total = total + ring_in[t, chunk].astype(jnp.float32)
            ring_out[t, chunk] = total.astype(jnp.bfloat16)
            if t == near:
                jump(q).start()
            elif t == 0:
                back_final(q).start()
            else:
                back_copy(t, q).start()

    @pl.loop(0, steps + LAG_OUT)
    def _(i):
        for k in range(PIECES):
            advance(i, 1, k)
            advance(i + LEAD, 0, k)

        if EARLY > 0 and near > 0:
            @pl.when(i == steps + 1)
            def _():
                scatter(near - 1)

        @pl.when((i >= LAG_MID) & (i < steps + LAG_MID))
        def _():
            bend(i - LAG_MID)

        @pl.when(i >= LAG_OUT)
        def _():
            project(i - LAG_OUT)

        if EARLY > 1 and near > 1:
            @pl.when(i == steps + 2)
            def _():
                scatter(near - 2)

        @pl.when(i == 0)
        def _():
            weights_all().wait_recv()

        @pl.when(i < last)
        def _():
            whole = gathered.at[:, i, other_lane]
            remote(whole, whole, core_send.at[0], core_recv.at[i], twin).wait_recv()

        @pl.when(i == last)
        def _():
            whole = gathered.at[:, last, other_far]
            remote(whole, whole, core_send.at[0], core_recv.at[last], twin).wait_recv()

        @pl.when(i < steps)
        def _():
            multiply(i)

    early = min(EARLY, near)
    scatter_first()
    far_steps = list(range(last - 1, near - 1, -1))
    near_steps = list(range(near - 1 - early, -1, -1))
    while far_steps or near_steps:
        if near_steps:
            scatter(near_steps.pop(0))
        if far_steps:
            scatter(far_steps.pop(0))

    def return_copy(to):
        return remote(
            final_rows.at[part_of(to, MOST)], returned.at[part_of(expert, MOST), mine],
            return_send.at[0], return_recv.at[0], (to, frm),
        )

    def return_all():
        return bulk((share - MOST) * half, return_send.at[0], return_recv.at[0])

    return_own = pltpu.make_async_copy(
        final_rows.at[part_of(grp, MOST)], returned.at[part_of(expert, MOST), mine], own_sem.at[2]
    )
    part_own().wait_recv()
    reach = piece // MOST
    for n in range(CHUNKS // 2):
        rows = pl.ds(pl.multiple_of(core * share + n * piece, piece), piece)
        other = pl.ds(share + n * piece, piece)
        chunk = pl.ds(n * piece, piece)
        total = parts[last, rows].astype(jnp.float32) + cross[last, other].astype(jnp.float32)
        for buffer, sem in ((last_in, last_recv), (far_in, jump_recv)):
            for way in range(2):
                arrival(buffer, sem, way, n).wait_recv()
                total = total + buffer[way, chunk].astype(jnp.float32)
        final_rows[chunk] = total.astype(jnp.bfloat16)

        @pl.loop(0, reach)
        def _(j):
            to = n * reach + lax.rem(grp + j, reach)

            @pl.when(to != grp)
            def _():
                return_copy(to).start()

            @pl.when(to == grp)
            def _():
                return_own.start()

    cot_all().wait_send()

    for copy in outs:
        copy.wait()

    for a in range(2):
        pick_all(a).wait_send()
    weights_all().wait_send()
    moved = (last * block + share) * half
    bulk(2 * moved, ring_send.at[0], ring_recv.at[0, 0, 0]).wait_send()
    bulk(2 * moved, core_send.at[0], core_recv.at[0]).wait_send()
    remote(cross, cross, part_send.at[0], part_recv.at[0], twin).wait_send()
    remote(x_send, x_recv, x_send_sem.at[0], x_recv_sem.at[0], mate).wait_send()
    slopes_all = slopes.at[:, :, pl.ds(0, hidden)]
    remote(slopes_all, slopes_all, slope_send.at[0], slope_recv.at[0], mate).wait_send()
    bulk(moved, back_send.at[0], back_recv.at[0, 0]).wait_send()
    return_own.wait()

    return_all().wait_send()
    return_all().wait_recv()
    back_ref[...] = returned[...]


def layer(query_in, key_in, value_in, cotangent, w_in, w_out, gates, chosen):
    levels = lax.axis_size("frm") // 2
    groups = lax.axis_size("grp")
    frames, blocks, features = query_in.shape
    local_rows = frames * blocks
    steps = levels // 2
    share = MOST * groups
    half = features // 2
    block = 2 * share
    hidden = w_in.shape[1]
    slots = MOST * chosen.shape[0]
    patches = blocks * groups * 2 * levels
    bf16 = jnp.bfloat16
    dma = pltpu.SemaphoreType.DMA
    vmem = pl.BlockSpec(memory_space=pltpu.VMEM)
    hbm = pl.BlockSpec(memory_space=pl.ANY)
    return pl.pallas_call(
        functools.partial(layer_kernel, levels, groups, patches),
        out_shape=(
            jax.ShapeDtypeStruct((HEADS, local_rows, local_rows), jnp.float32),
            jax.ShapeDtypeStruct((slots, local_rows), bf16),
            jax.ShapeDtypeStruct((local_rows, features), bf16),
            jax.ShapeDtypeStruct((local_rows, features), bf16),
            jax.ShapeDtypeStruct((local_rows, features), bf16),
            jax.ShapeDtypeStruct((local_rows, features), bf16),
            jax.ShapeDtypeStruct((slots, features), bf16),
        ),
        in_specs=[hbm] * 6 + [vmem] * 2,
        out_specs=(hbm,) * 6 + (vmem,),
        scratch_shapes=[
            pltpu.VMEM((local_rows, features), bf16),
            pltpu.VMEM((local_rows, features), bf16),
            pltpu.VMEM((local_rows, features), bf16),
            pltpu.VMEM((local_rows, features), bf16),
            pltpu.VMEM((local_rows, features), bf16),
            pltpu.VMEM((HEADS, local_rows, local_rows), jnp.float32),
            pltpu.VMEM((slots, local_rows), bf16),
            pltpu.VMEM((2, slots, features), bf16),
            pltpu.VMEM((slots, features), bf16),
            pltpu.VMEM((share, half), bf16),
            pltpu.VMEM((2, steps, 2 * block, half), bf16),
            pltpu.VMEM((half, 2 * hidden), bf16),
            pltpu.VMEM((2 * hidden, half), bf16),
            pltpu.VMEM((steps, 2, 2 * block, hidden), jnp.float32),
            pltpu.VMEM((steps, 2, 2 * block, hidden), bf16),
            pltpu.VMEM((steps, 2, 2 * block, hidden), bf16),
            pltpu.VMEM((steps, 2 * block, 2 * hidden), bf16),
            pltpu.VMEM((steps, 2 * block, half), bf16),
            pltpu.VMEM((steps, block, half), bf16),
            pltpu.VMEM((steps, block, half), bf16),
            pltpu.VMEM((steps, block, half), bf16),
            pltpu.VMEM((2, share, half), bf16),
            pltpu.VMEM((2, share, half), bf16),
            pltpu.VMEM((32, 128, 128), jnp.float32),
            dma((3,)), dma((3,)), dma((6,)), dma((3,)), dma((1,)), dma((1,)),
            dma((1,)), dma((steps, 2, PIECES)), dma((1,)), dma((steps,)),
            dma((1,)), dma((steps,)), dma((1,)), dma((steps,)),
            dma((1,)), dma((steps + 1,)), dma((1,)), dma((steps, CHUNKS)), dma((2, CHUNKS // 2)), dma((2, CHUNKS // 2)),
            dma((1,)), dma((1,)), dma((2,)), dma((2,)), dma((1,)), dma((1,)),
        ],
        compiler_params=pltpu.CompilerParams(
            collective_id=0, has_side_effects=True
        ),
        name="layer",
    )(query_in, key_in, value_in, cotangent, w_in, w_out, gates, chosen)


def attention_kernel(
    query_ref, key_ref, value_ref, probs_ref, onehot_ref, stream_ref, back_ref,
    grad_query_ref, grad_key_ref, grad_value_ref,
):
    frames, blocks, width = grad_query_ref.shape
    local_rows = frames * blocks
    heads = probs_ref.shape[0]
    head_dim = width // heads
    scaling = head_dim ** (-0.5)
    added = lax.dot_general(
        onehot_ref[...], back_ref[...], TN_DIMS, preferred_element_type=jnp.float32
    )
    stream = (stream_ref[...].astype(jnp.float32) + added).astype(jnp.bfloat16)
    cols = [slice(n * head_dim, (n + 1) * head_dim) for n in range(heads)]

    def store(ref, n, values):
        ref[:, :, cols[n]] = values.astype(jnp.bfloat16).reshape(frames, blocks, head_dim)

    grad_probs = [
        lax.dot_general(stream[:, c], value_ref[:, c], NT_DIMS, preferred_element_type=jnp.float32) for c in cols
    ]
    grad_values = [
        lax.dot_general(
            probs_ref[n].astype(jnp.bfloat16), stream[:, c], TN_DIMS, preferred_element_type=jnp.float32
        ) for n, c in enumerate(cols)
    ]
    grad_scores = []
    for n in range(heads):
        weighted = probs_ref[n] * grad_probs[n]
        centre = jnp.sum(weighted, axis=1, keepdims=True)
        grad_scores.append((probs_ref[n] * (grad_probs[n] - centre)).astype(jnp.bfloat16))
    for n in range(heads):
        store(grad_value_ref, n, grad_values[n])
    grad_queries = [
        jnp.dot(grad_scores[n], key_ref[:, c], preferred_element_type=jnp.float32) * scaling
        for n, c in enumerate(cols)
    ]
    grad_keys = [
        lax.dot_general(grad_scores[n], query_ref[:, c], TN_DIMS, preferred_element_type=jnp.float32) * scaling
        for n, c in enumerate(cols)
    ]
    for n in range(heads):
        store(grad_query_ref, n, grad_queries[n])
        store(grad_key_ref, n, grad_keys[n])


def attention_back(frames, query, key, value, probs, onehot, stream, back):
    local_rows, features = query.shape
    blocks = local_rows // frames
    slots = onehot.shape[0]
    width = features // WIDE
    rows = pl.BlockSpec((local_rows, width), lambda n: (0, n))
    whole = pl.BlockSpec((frames, blocks, width), lambda n: (0, 0, n))
    return pl.pallas_call(
        attention_kernel,
        grid=(WIDE,),
        out_shape=(jax.ShapeDtypeStruct((frames, blocks, features), jnp.bfloat16),) * 3,
        in_specs=[
            rows, rows, rows,
            pl.BlockSpec((HEADS // WIDE, local_rows, local_rows), lambda n: (n, 0, 0)),
            pl.BlockSpec((slots, local_rows), lambda n: (0, 0)),
            rows,
            pl.BlockSpec((slots, width), lambda n: (0, n)),
        ],
        out_specs=(whole,) * 3,
        compiler_params=pltpu.CompilerParams(dimension_semantics=("arbitrary",)),
        name="attention_back",
    )(query, key, value, probs, onehot, stream, back)


def body(query_in, key_in, value_in, cotangent, w_in, w_out, gate_probs, chosen):
    probs, onehot, stream, query, key, value, back = layer(
        query_in, key_in, value_in, cotangent, w_in[0], w_out[0], gate_probs, chosen
    )
    return attention_back(query_in.shape[0], query, key, value, probs, onehot, stream, back)


def solution(mesh):
    return jax.shard_map(
        body,
        mesh=mesh,
        in_specs=(
            P(None, ("grp", "frm"), None),
            P(None, ("grp", "frm"), None),
            P(None, ("grp", "frm"), None),
            P("frm", "grp", None),
            P("grp", None, "frm"),
            P("grp", "frm", None),
            P(),
            P(),
        ),
        out_specs=(
            P(None, ("grp", "frm"), None),
            P(None, ("grp", "frm"), None),
            P(None, ("grp", "frm"), None),
        ),
        check_vma=False,
    )
```

```python
import functools

import jax
import jax.numpy as jnp
from jax import lax
from jax.experimental import pallas as pl
from jax.experimental.pallas import tpu as pltpu
from jax.sharding import PartitionSpec as P

HEADS = 16
MOST = 2
MESH = pl.DeviceIdType.MESH

root_half = 0.7071067811865476
inv_root_tau = 0.3989422804014327


def gelu_slope(pre_act):
    normal_cdf = 0.5 * (1.0 + lax.erf(pre_act * root_half))
    density = jnp.exp(-0.5 * pre_act * pre_act) * inv_root_tau
    return normal_cdf + pre_act * density


NT_DIMS = (((1,), (1,)), ((), ()))
TN_DIMS = (((0,), (0,)), ((), ()))
LAG_MID = 2
LAG_OUT = 4
LEAD = 1
PIECES = 4
CHUNKS = 4
WIDE = 2
EARLY = 2


def bits(n):
    assert n & (n - 1) == 0
    return n.bit_length() - 1


def onehot_rows(chosen, gates, myself, blocks, patches, local_rows):
    experts_total, cap = chosen.shape
    slots = MOST * experts_total

    def twice(values):
        spread = jnp.broadcast_to(values[:, None, :], (experts_total, MOST, cap))
        return spread.reshape(slots, cap)

    token = twice(chosen)
    gate = twice(gates)
    patch = token & (patches - 1)
    frame = lax.shift_right_logical(token, bits(patches))
    holder = lax.shift_right_logical(patch, bits(blocks))
    place = frame * blocks + (patch & (blocks - 1))
    order = lax.broadcasted_iota(jnp.int32, (slots, cap), 1)
    key = (order * local_rows + place).astype(jnp.float32)
    owned = holder == myself
    beyond = float(cap * local_rows)
    low = jnp.min(jnp.where(owned, key, beyond), axis=1, keepdims=True)
    high = jnp.max(jnp.where(owned, key, -1.0), axis=1, keepdims=True)
    odd = (lax.broadcasted_iota(jnp.int32, (slots, 1), 0) & 1) == 1
    key_at = jnp.where(odd, high, low)
    present = jnp.where(odd, (high > low).astype(jnp.float32), (low < beyond).astype(jnp.float32))
    place_at = key_at - jnp.floor(key_at * (1.0 / local_rows)) * local_rows
    gate_at = jnp.sum(jnp.where(owned & (key == key_at), gate, 0.0), axis=1, keepdims=True)
    row = lax.broadcasted_iota(jnp.int32, (slots, local_rows), 1).astype(jnp.float32)
    hit = jnp.where((row == place_at) & (present > 0.5), 1.0, 0.0)
    return hit.astype(jnp.bfloat16), gate_at


def layer_kernel(
    levels, groups, patches,
    query_ref, key_ref, value_ref, cot_ref, w_in_ref, w_out_ref, gates_ref, chosen_ref,
    probs_ref, onehot_ref, stream_ref, query_rows_ref, key_rows_ref, value_rows_ref, back_ref,
    query, key, value, mixed, cot_rows, probs_all, onehot_all, picked, returned, final_rows,
    gathered, w1, w2, own, x_send, x_recv, slopes, parts, cross, ring_in, ring_out,
    last_in, far_in, gauge,
    local_sem, load_sem, out_sem, own_sem, weight_send, weight_recv,
    ring_send, ring_recv, core_send, core_recv, x_send_sem, x_recv_sem,
    slope_send, slope_recv, part_send, part_recv, back_send, back_recv, last_recv, jump_recv,
    cot_send, cot_recv, pick_send, pick_recv, return_send, return_recv,
):
    steps = levels // 2
    last = steps - 1
    near = steps * 5 // 8
    columns = 2 * levels
    frames, blocks, features = query_ref.shape
    local_rows = frames * blocks
    head_dim = features // HEADS
    half = features // 2
    share = MOST * groups
    block = 2 * share
    hidden = w_in_ref.shape[1]
    grp = lax.axis_index("grp")
    frm = lax.axis_index("frm")
    side = lax.rem(grp, 2)
    expert = lax.div(grp, 2)
    core = lax.rem(frm, 2)
    level = lax.div(frm, 2)
    turn = 1 - 2 * core
    ahead = (grp, lax.rem(level + turn + levels, levels) * 2 + core)
    behind = (grp, lax.rem(level - turn + levels, levels) * 2 + core)
    twin = (grp, frm + turn)
    mate = (grp + 1 - 2 * side, frm)

    def remote(src, dst, send, recv, device):
        return pltpu.make_async_remote_copy(
            src_ref=src, dst_ref=dst, send_sem=send, recv_sem=recv, device_id=device, device_id_type=MESH
        )

    def bulk(elements, send, recv):
        lines = elements // (2 * gauge.shape[2])
        many = max(n for n in range(1, gauge.shape[0] + 1) if lines % (8 * n) == 0)
        assert lines * 2 * gauge.shape[2] == elements and lines // many <= gauge.shape[1]
        ref = gauge.at[pl.ds(0, many), pl.ds(0, lines // many)]
        return remote(ref, ref, send, recv, twin)

    def part_of(index, size):
        return pl.ds(pl.multiple_of(index * size, size), size)

    barrier = pltpu.get_barrier_semaphore()

    @pl.loop(1, columns)
    def _(d):
        pl.semaphore_signal(
            barrier, inc=1, device_id=(grp, lax.rem(frm + d, columns)), device_id_type=MESH
        )

    @pl.loop(1, groups)
    def _(d):
        for k in range(2):
            pl.semaphore_signal(
                barrier, inc=1, device_id=(lax.rem(grp + d, groups), frm + k * turn), device_id_type=MESH
            )

    mine = part_of(side, half)
    theirs = part_of(1 - side, half)
    here = part_of(core, share)
    there = part_of(1 - core, share)
    lane = part_of(core, block)
    other_lane = part_of(1 - core, block)
    lane_part = pl.ds(pl.multiple_of(core * (block + share), share), share)
    far = pl.ds(pl.multiple_of(block + core * share, share), share)
    other_far = pl.ds(pl.multiple_of(block + (1 - core) * share, share), share)

    pl.semaphore_wait(barrier, columns - 1 + 2 * (groups - 1))

    def cot_copy(other):
        return remote(
            cot_ref.at[0, part_of(other, blocks)], cot_rows.at[part_of(frm, blocks)],
            cot_send.at[0], cot_recv.at[0], (grp, other),
        )

    def cot_all():
        return bulk((columns - 1) * blocks * features, cot_send.at[0], cot_recv.at[0])

    @pl.loop(0, levels - 1)
    def _(k):
        away = steps - lax.div(k + 1, 2)
        to = lax.rem(level + levels + (2 * lax.rem(k, 2) - 1) * away, levels)
        cot_copy(2 * to + core).start()
        cot_copy(2 * to + 1 - core).start()

    cot_copy(frm + turn).start()
    weights = [
        remote(w_in_ref.at[theirs], w1.at[:, pl.ds(hidden, hidden)], weight_send.at[0], weight_recv.at[0], mate),
        remote(w_out_ref.at[:, theirs], w2.at[pl.ds(hidden, hidden)], weight_send.at[0], weight_recv.at[0], mate),
    ]
    for copy in weights:
        copy.start()

    def weights_all():
        return remote(w1, w1, weight_send.at[0], weight_recv.at[0], mate)


    inputs = ((query_ref, query), (key_ref, key), (value_ref, value))

    @pl.loop(0, frames)
    def _(f):
        for n, (src, dst) in enumerate(inputs):
            pltpu.make_async_copy(src.at[f], dst.at[part_of(f, blocks)], load_sem.at[n]).start()

    local = [
        pltpu.make_async_copy(w_in_ref.at[mine], w1.at[:, pl.ds(0, hidden)], local_sem.at[0]),
        pltpu.make_async_copy(w_out_ref.at[:, mine], w2.at[pl.ds(0, hidden)], local_sem.at[1]),
        pltpu.make_async_copy(
            cot_ref.at[0, part_of(frm, blocks)], cot_rows.at[part_of(frm, blocks)], local_sem.at[2]
        ),
    ]
    for copy in local:
        copy.start()
    myself = grp * columns + frm
    onehot, gate_at = onehot_rows(chosen_ref[...], gates_ref[...], myself, blocks, patches, local_rows)
    onehot_all[...] = onehot

    for n, (_, dst) in enumerate(inputs):
        pltpu.make_async_copy(dst, dst, load_sem.at[n]).wait()
    row_patch = lax.broadcasted_iota(jnp.int32, (local_rows, local_rows), 0) & (blocks - 1)
    column_patch = lax.broadcasted_iota(jnp.int32, (local_rows, local_rows), 1) & (blocks - 1)
    same = row_patch == column_patch
    scaling = head_dim ** (-0.5)
    together = 4

    @pl.loop(0, HEADS // together)
    def _(n):
        for m in range(together):
            head = n * together + m
            cols = part_of(head, head_dim)
            scores = lax.dot_general(
                query[:, cols], key[:, cols], NT_DIMS, preferred_element_type=jnp.float32
            ) * scaling
            scores = jnp.where(same, scores, -1e30)
            raised = jnp.exp(scores - jnp.max(scores, axis=1, keepdims=True))
            probs = raised / jnp.sum(raised, axis=1, keepdims=True)
            probs_all[head] = probs
            mixed[:, cols] = jnp.dot(
                probs.astype(jnp.bfloat16), value[:, cols], preferred_element_type=jnp.float32
            ).astype(jnp.bfloat16)

    outs = [
        pltpu.make_async_copy(src, dst, out_sem.at[n])
        for n, (src, dst) in enumerate((
            (probs_all, probs_ref), (onehot_all, onehot_ref), (query, query_rows_ref),
            (key, key_rows_ref), (value, value_rows_ref), (cot_rows, stream_ref),
        ))
    ]

    def pick_copy(a, d, k):
        to = lax.rem(grp + d, groups)
        return remote(
            picked.at[a, part_of(lax.div(to, 2), MOST), part_of(lax.rem(to, 2), half)],
            gathered.at[a, last, pl.ds(pl.multiple_of(core * share + grp * MOST, MOST), MOST)],
            pick_send.at[a], pick_recv.at[a], (to, frm + k * turn),
        )

    def pick_all(a):
        return bulk((block - MOST) * half, pick_send.at[a], pick_recv.at[a])

    def pick_own(a):
        return pltpu.make_async_copy(
            picked.at[a, part_of(expert, MOST), part_of(side, half)],
            gathered.at[a, last, pl.ds(pl.multiple_of(core * share + grp * MOST, MOST), MOST)],
            own_sem.at[a],
        )

    def send_picked(a):
        @pl.loop(1, groups)
        def _(d):
            for k in range(2):
                pick_copy(a, d, k).start()

        pick_copy(a, 0, 1).start()
        pick_own(a).start()

    def take_picked(a):
        pick_own(a).wait()
        pick_all(a).wait_recv()
        for k in range(PIECES):
            ring_first(a, k).start()

    picked[0] = jnp.dot(onehot, mixed[...], preferred_element_type=jnp.float32).astype(jnp.bfloat16)
    send_picked(0)
    for copy in outs[:5]:
        copy.start()

    slab = block // PIECES

    def lane_slab(k):
        return pl.ds(pl.multiple_of(core * block + k * slab, slab), slab)

    def ring(t, a, k):
        return remote(
            gathered.at[a, lax.max(t - 1, 0), lane_slab(k)], gathered.at[a, t, lane_slab(k)],
            ring_send.at[0], ring_recv.at[t, a, k], ahead,
        )

    def ring_first(a, k):
        return remote(
            gathered.at[a, last, pl.ds(k * slab, slab)], gathered.at[a, 0, lane_slab(k)],
            ring_send.at[0], ring_recv.at[0, a, k], ahead,
        )

    def ring_last(a):
        return remote(
            gathered.at[a, last - 1, lane_part], gathered.at[a, last, far],
            ring_send.at[0], ring_recv.at[last, a, 0], ahead,
        )

    def core_copy(t, a, k):
        return remote(
            gathered.at[a, t, lane_slab(k)], gathered.at[a, t, lane_slab(k)],
            core_send.at[0], core_recv.at[t], twin,
        )

    def core_last(a):
        return remote(
            gathered.at[a, last, far], gathered.at[a, last, far],
            core_send.at[0], core_recv.at[last], twin,
        )

    def advance(t, a, k):
        @pl.when(t < last)
        def _():
            ring(t, a, k).wait_recv()

            @pl.when(t < last - 1)
            def _():
                ring(t + 1, a, k).start()

            if k == PIECES - 1:
                @pl.when(t == last - 1)
                def _():
                    ring_last(a).start()

            core_copy(t, a, k).start()

        if k == 0:
            @pl.when(t == last)
            def _():
                ring_last(a).wait_recv()
                core_last(a).start()

    def x_copy(t):
        return remote(x_send.at[t], x_recv.at[t], x_send_sem.at[0], x_recv_sem.at[t], mate)

    def slope_copy(t):
        return remote(
            slopes.at[t, :, pl.ds(0, hidden)], slopes.at[t, :, pl.ds(hidden, hidden)],
            slope_send.at[0], slope_recv.at[t], mate,
        )

    def part_copy(t):
        return remote(parts.at[t, other_lane], cross.at[t], part_send.at[0], part_recv.at[t], twin)

    def part_own():
        return remote(
            parts.at[last, there], cross.at[last, pl.ds(share, share)],
            part_send.at[0], part_recv.at[steps], twin,
        )

    def part_last():
        return remote(
            parts.at[last, other_far], cross.at[last, pl.ds(0, share)],
            part_send.at[0], part_recv.at[last], twin,
        )

    take_picked(0)
    local[2].wait()

    cot_all().wait_recv()

    picked_cot = jnp.dot(onehot_all[...], cot_rows[...], preferred_element_type=jnp.float32)
    picked[1] = (gate_at * picked_cot).astype(jnp.bfloat16)
    send_picked(1)
    for n in range(LEAD):
        for k in range(PIECES):
            advance(jnp.int32(n), 0, k)
    outs[5].start()
    for copy in local[:2]:
        copy.wait()
    take_picked(1)

    def multiply(t):
        pre = jnp.dot(gathered[0, t], w1[...], preferred_element_type=jnp.float32)
        own[t, 0] = pre[:, :hidden]
        x_send[t, 0] = pre[:, hidden:].astype(jnp.bfloat16)
        back = lax.dot_general(gathered[1, t], w2[...], NT_DIMS, preferred_element_type=jnp.float32)
        own[t, 1] = back[:, :hidden]
        x_send[t, 1] = back[:, hidden:].astype(jnp.bfloat16)
        x_copy(t).start()

    def bend(t):
        x_copy(t).wait_recv()
        pre = own[t, 0] + x_recv[t, 0].astype(jnp.float32)
        back = own[t, 1] + x_recv[t, 1].astype(jnp.float32)
        slopes[t, :, pl.ds(0, hidden)] = (back * gelu_slope(pre)).astype(jnp.bfloat16)
        slope_copy(t).start()

    def project(t):
        slope_copy(t).wait_recv()
        parts[t] = lax.dot_general(
            slopes[t], w1[...], NT_DIMS, preferred_element_type=jnp.float32
        ).astype(jnp.bfloat16)

        @pl.when(t < last)
        def _():
            part_copy(t).start()

        @pl.when(t == last)
        def _():
            part_last().start()
            part_own().start()

    piece = block // CHUNKS

    def chunk_of(q):
        where = (1 - core) if q < CHUNKS // 2 else core
        return where * share + (q % (CHUNKS // 2)) * piece

    def back_copy(t, q):
        chunk = pl.ds(pl.multiple_of(chunk_of(q), piece), piece)
        return remote(
            ring_out.at[t, chunk], ring_in.at[t - 1, chunk], back_send.at[0], back_recv.at[t, q], behind
        )

    def back_final(q):
        chunk = pl.ds(pl.multiple_of(chunk_of(q), piece), piece)
        n = q % (CHUNKS // 2)
        owner = (1 - core) if q < CHUNKS // 2 else core
        return remote(
            ring_out.at[0, chunk], last_in.at[core, pl.ds(n * piece, piece)],
            back_send.at[0], last_recv.at[core, n], (grp, behind[1] - core + owner),
        )

    def jump(q):
        chunk = pl.ds(pl.multiple_of(chunk_of(q), piece), piece)
        n = q % (CHUNKS // 2)
        owner = (1 - core) if q < CHUNKS // 2 else core
        home = lax.rem(level + levels - turn * (near + 1), levels)
        return remote(
            ring_out.at[near, chunk], far_in.at[core, pl.ds(n * piece, piece)],
            back_send.at[0], jump_recv.at[core, n], (grp, 2 * home + owner),
        )

    def arrival(buffer, sem, way, n):
        ref = buffer.at[way, pl.ds(n * piece, piece)]
        return remote(ref, ref, back_send.at[0], sem.at[way, n], twin)

    def scatter_first():
        part_last().wait_recv()
        for q in range(CHUNKS // 2, CHUNKS):
            chunk = pl.ds(pl.multiple_of(chunk_of(q), piece), piece)
            source = pl.ds(pl.multiple_of(block + chunk_of(q), piece), piece)
            other = pl.ds((q - CHUNKS // 2) * piece, piece)
            total = parts[last, source].astype(jnp.float32) + cross[last, other].astype(jnp.float32)
            ring_out[last, chunk] = total.astype(jnp.bfloat16)
            back_copy(last, q).start()

    def scatter(t):
        part_copy(t).wait_recv()
        for q in range(CHUNKS):
            chunk = pl.ds(pl.multiple_of(chunk_of(q), piece), piece)
            source = pl.ds(pl.multiple_of(core * block + chunk_of(q), piece), piece)
            total = parts[t, source].astype(jnp.float32) + cross[t, chunk].astype(jnp.float32)
            begun = t == near - 1 or (t == last - 1 and q < CHUNKS // 2)
            if not begun:
                back_copy(t + 1, q).wait_recv()
                total = total + ring_in[t, chunk].astype(jnp.float32)
            ring_out[t, chunk] = total.astype(jnp.bfloat16)
            if t == near:
                jump(q).start()
            elif t == 0:
                back_final(q).start()
            else:
                back_copy(t, q).start()

    @pl.loop(0, steps + LAG_OUT)
    def _(i):
        for k in range(PIECES):
            advance(i, 1, k)
            advance(i + LEAD, 0, k)

        if EARLY > 0 and near > 0:
            @pl.when(i == steps + 1)
            def _():
                scatter(near - 1)

        @pl.when((i >= LAG_MID) & (i < steps + LAG_MID))
        def _():
            bend(i - LAG_MID)

        @pl.when(i >= LAG_OUT)
        def _():
            project(i - LAG_OUT)

        if EARLY > 1 and near > 1:
            @pl.when(i == steps + 2)
            def _():
                scatter(near - 2)

        @pl.when(i == 0)
        def _():
            weights_all().wait_recv()

        @pl.when(i < last)
        def _():
            whole = gathered.at[:, i, other_lane]
            remote(whole, whole, core_send.at[0], core_recv.at[i], twin).wait_recv()

        @pl.when(i == last)
        def _():
            whole = gathered.at[:, last, other_far]
            remote(whole, whole, core_send.at[0], core_recv.at[last], twin).wait_recv()

        @pl.when(i < steps)
        def _():
            multiply(i)

    early = min(EARLY, near)
    scatter_first()
    far_steps = list(range(last - 1, near - 1, -1))
    near_steps = list(range(near - 1 - early, -1, -1))
    while far_steps or near_steps:
        if near_steps:
            scatter(near_steps.pop(0))
        if far_steps:
            scatter(far_steps.pop(0))

    def return_copy(to):
        return remote(
            final_rows.at[part_of(to, MOST)], returned.at[part_of(expert, MOST), mine],
            return_send.at[0], return_recv.at[0], (to, frm),
        )

    def return_all():
        return bulk((share - MOST) * half, return_send.at[0], return_recv.at[0])

    return_own = pltpu.make_async_copy(
        final_rows.at[part_of(grp, MOST)], returned.at[part_of(expert, MOST), mine], own_sem.at[2]
    )
    part_own().wait_recv()
    reach = piece // MOST
    for n in range(CHUNKS // 2):
        rows = pl.ds(pl.multiple_of(core * share + n * piece, piece), piece)
        other = pl.ds(share + n * piece, piece)
        chunk = pl.ds(n * piece, piece)
        total = parts[last, rows].astype(jnp.float32) + cross[last, other].astype(jnp.float32)
        for buffer, sem in ((last_in, last_recv), (far_in, jump_recv)):
            for way in range(2):
                arrival(buffer, sem, way, n).wait_recv()
                total = total + buffer[way, chunk].astype(jnp.float32)
        final_rows[chunk] = total.astype(jnp.bfloat16)

        @pl.loop(0, reach)
        def _(j):
            to = n * reach + lax.rem(grp + j, reach)

            @pl.when(to != grp)
            def _():
                return_copy(to).start()

            @pl.when(to == grp)
            def _():
                return_own.start()

    cot_all().wait_send()

    for copy in outs:
        copy.wait()

    for a in range(2):
        pick_all(a).wait_send()
    weights_all().wait_send()
    moved = (last * block + share) * half
    bulk(2 * moved, ring_send.at[0], ring_recv.at[0, 0, 0]).wait_send()
    bulk(2 * moved, core_send.at[0], core_recv.at[0]).wait_send()
    remote(cross, cross, part_send.at[0], part_recv.at[0], twin).wait_send()
    remote(x_send, x_recv, x_send_sem.at[0], x_recv_sem.at[0], mate).wait_send()
    slopes_all = slopes.at[:, :, pl.ds(0, hidden)]
    remote(slopes_all, slopes_all, slope_send.at[0], slope_recv.at[0], mate).wait_send()
    bulk(moved, back_send.at[0], back_recv.at[0, 0]).wait_send()
    return_own.wait()

    return_all().wait_send()
    return_all().wait_recv()
    back_ref[...] = returned[...]


def layer(query_in, key_in, value_in, cotangent, w_in, w_out, gates, chosen):
    levels = lax.axis_size("frm") // 2
    groups = lax.axis_size("grp")
    frames, blocks, features = query_in.shape
    local_rows = frames * blocks
    steps = levels // 2
    share = MOST * groups
    half = features // 2
    block = 2 * share
    hidden = w_in.shape[1]
    slots = MOST * chosen.shape[0]
    patches = blocks * groups * 2 * levels
    bf16 = jnp.bfloat16
    dma = pltpu.SemaphoreType.DMA
    vmem = pl.BlockSpec(memory_space=pltpu.VMEM)
    hbm = pl.BlockSpec(memory_space=pl.ANY)
    return pl.pallas_call(
        functools.partial(layer_kernel, levels, groups, patches),
        out_shape=(
            jax.ShapeDtypeStruct((HEADS, local_rows, local_rows), jnp.float32),
            jax.ShapeDtypeStruct((slots, local_rows), bf16),
            jax.ShapeDtypeStruct((local_rows, features), bf16),
            jax.ShapeDtypeStruct((local_rows, features), bf16),
            jax.ShapeDtypeStruct((local_rows, features), bf16),
            jax.ShapeDtypeStruct((local_rows, features), bf16),
            jax.ShapeDtypeStruct((slots, features), bf16),
        ),
        in_specs=[hbm] * 6 + [vmem] * 2,
        out_specs=(hbm,) * 6 + (vmem,),
        scratch_shapes=[
            pltpu.VMEM((local_rows, features), bf16),
            pltpu.VMEM((local_rows, features), bf16),
            pltpu.VMEM((local_rows, features), bf16),
            pltpu.VMEM((local_rows, features), bf16),
            pltpu.VMEM((local_rows, features), bf16),
            pltpu.VMEM((HEADS, local_rows, local_rows), jnp.float32),
            pltpu.VMEM((slots, local_rows), bf16),
            pltpu.VMEM((2, slots, features), bf16),
            pltpu.VMEM((slots, features), bf16),
            pltpu.VMEM((share, half), bf16),
            pltpu.VMEM((2, steps, 2 * block, half), bf16),
            pltpu.VMEM((half, 2 * hidden), bf16),
            pltpu.VMEM((2 * hidden, half), bf16),
            pltpu.VMEM((steps, 2, 2 * block, hidden), jnp.float32),
            pltpu.VMEM((steps, 2, 2 * block, hidden), bf16),
            pltpu.VMEM((steps, 2, 2 * block, hidden), bf16),
            pltpu.VMEM((steps, 2 * block, 2 * hidden), bf16),
            pltpu.VMEM((steps, 2 * block, half), bf16),
            pltpu.VMEM((steps, block, half), bf16),
            pltpu.VMEM((steps, block, half), bf16),
            pltpu.VMEM((steps, block, half), bf16),
            pltpu.VMEM((2, share, half), bf16),
            pltpu.VMEM((2, share, half), bf16),
            pltpu.VMEM((32, 128, 128), jnp.float32),
            dma((3,)), dma((3,)), dma((6,)), dma((3,)), dma((1,)), dma((1,)),
            dma((1,)), dma((steps, 2, PIECES)), dma((1,)), dma((steps,)),
            dma((1,)), dma((steps,)), dma((1,)), dma((steps,)),
            dma((1,)), dma((steps + 1,)), dma((1,)), dma((steps, CHUNKS)), dma((2, CHUNKS // 2)), dma((2, CHUNKS // 2)),
            dma((1,)), dma((1,)), dma((2,)), dma((2,)), dma((1,)), dma((1,)),
        ],
        compiler_params=pltpu.CompilerParams(
            collective_id=0, has_side_effects=True
        ),
        name="layer",
    )(query_in, key_in, value_in, cotangent, w_in, w_out, gates, chosen)


def attention_kernel(
    query_ref, key_ref, value_ref, probs_ref, onehot_ref, stream_ref, back_ref,
    grad_query_ref, grad_key_ref, grad_value_ref,
):
    frames, blocks, width = grad_query_ref.shape
    local_rows = frames * blocks
    heads = probs_ref.shape[0]
    head_dim = width // heads
    scaling = head_dim ** (-0.5)
    added = lax.dot_general(
        onehot_ref[...], back_ref[...], TN_DIMS, preferred_element_type=jnp.float32
    )
    stream = (stream_ref[...].astype(jnp.float32) + added).astype(jnp.bfloat16)
    cols = [slice(n * head_dim, (n + 1) * head_dim) for n in range(heads)]

    def store(ref, n, values):
        ref[:, :, cols[n]] = values.astype(jnp.bfloat16).reshape(frames, blocks, head_dim)

    grad_probs = [
        lax.dot_general(stream[:, c], value_ref[:, c], NT_DIMS, preferred_element_type=jnp.float32) for c in cols
    ]
    grad_values = [
        lax.dot_general(
            probs_ref[n].astype(jnp.bfloat16), stream[:, c], TN_DIMS, preferred_element_type=jnp.float32
        ) for n, c in enumerate(cols)
    ]
    grad_scores = []
    for n in range(heads):
        weighted = probs_ref[n] * grad_probs[n]
        centre = jnp.sum(weighted, axis=1, keepdims=True)
        grad_scores.append((probs_ref[n] * (grad_probs[n] - centre)).astype(jnp.bfloat16))
    for n in range(heads):
        store(grad_value_ref, n, grad_values[n])
    grad_queries = [
        jnp.dot(grad_scores[n], key_ref[:, c], preferred_element_type=jnp.float32) * scaling
        for n, c in enumerate(cols)
    ]
    grad_keys = [
        lax.dot_general(grad_scores[n], query_ref[:, c], TN_DIMS, preferred_element_type=jnp.float32) * scaling
        for n, c in enumerate(cols)
    ]
    for n in range(heads):
        store(grad_query_ref, n, grad_queries[n])
        store(grad_key_ref, n, grad_keys[n])


def attention_back(frames, query, key, value, probs, onehot, stream, back):
    local_rows, features = query.shape
    blocks = local_rows // frames
    slots = onehot.shape[0]
    width = features // WIDE
    rows = pl.BlockSpec((local_rows, width), lambda n: (0, n))
    whole = pl.BlockSpec((frames, blocks, width), lambda n: (0, 0, n))
    return pl.pallas_call(
        attention_kernel,
        grid=(WIDE,),
        out_shape=(jax.ShapeDtypeStruct((frames, blocks, features), jnp.bfloat16),) * 3,
        in_specs=[
            rows, rows, rows,
            pl.BlockSpec((HEADS // WIDE, local_rows, local_rows), lambda n: (n, 0, 0)),
            pl.BlockSpec((slots, local_rows), lambda n: (0, 0)),
            rows,
            pl.BlockSpec((slots, width), lambda n: (0, n)),
        ],
        out_specs=(whole,) * 3,
        compiler_params=pltpu.CompilerParams(dimension_semantics=("arbitrary",)),
        name="attention_back",
    )(query, key, value, probs, onehot, stream, back)


def body(query_in, key_in, value_in, cotangent, w_in, w_out, gate_probs, chosen):
    probs, onehot, stream, query, key, value, back = layer(
        query_in, key_in, value_in, cotangent, w_in[0], w_out[0], gate_probs, chosen
    )
    return attention_back(query_in.shape[0], query, key, value, probs, onehot, stream, back)


def solution(mesh):
    return jax.shard_map(
        body,
        mesh=mesh,
        in_specs=(
            P(None, ("grp", "frm"), None),
            P(None, ("grp", "frm"), None),
            P(None, ("grp", "frm"), None),
            P("frm", "grp", None),
            P("grp", None, "frm"),
            P("grp", "frm", None),
            P(),
            P(),
        ),
        out_specs=(
            P(None, ("grp", "frm"), None),
            P(None, ("grp", "frm"), None),
            P(None, ("grp", "frm"), None),
        ),
        check_vma=False,
    )
```
